256 devices in a mesh: region: 8 (over x, core), patch: 32 (over y, z).
Axes of the slice: x: 4, y: 4, z: 8, core: 2. Of those that a mesh axis runs over, the one named last changes fastest.
Arguments:
- nodes: bfloat16 [65536, 512], P(('region', 'patch')), may hold values from -6 to 6
- edges: bfloat16 [262144, 512], P(('region', 'patch')), may hold values from -6 to 6
- node_cotan: bfloat16 [65536, 512], P(('region', 'patch')), may hold values from -6 to 6
- edge_cotan: bfloat16 [262144, 512], P(('region', 'patch')), may hold values from -6 to 6
- edge_inner: bfloat16 [1536, 512], replicated, may hold values from -0.15625 to 0.15625
- edge_outer: bfloat16 [512, 512], replicated, may hold values from -0.25 to 0.25
- node_inner: bfloat16 [1024, 512], replicated, may hold values from -0.1875 to 0.1875
- node_outer: bfloat16 [512, 512], replicated, may hold values from -0.25 to 0.25
- edge_shift: float32 [512], replicated, may hold values from -4 to 4
- edge_offset: float32 [512], replicated, may hold values from -4 to 4
- edge_gain: float32 [512], replicated, may hold values from 0.5 to 1.5
- node_shift: float32 [512], replicated, may hold values from -4 to 4
- node_offset: float32 [512], replicated, may hold values from -4 to 4
- node_gain: float32 [512], replicated, may hold values from 0.5 to 1.5
- send_rows: int32 [8, 32, 2, 32], P('region', 'patch'), may hold values from -1 to 255, as said below
- senders: int32 [262144], P(('region', 'patch')), may hold values from 0 to 319, as said below
- receivers: int32 [262144], P(('region', 'patch')), may hold values from 0 to 255
Outputs:
- grad_nodes: float32 [65536, 512], P(('region', 'patch'))
- grad_edges: bfloat16 [262144, 512], P(('region', 'patch'))
- grad_weights: float32 [1835008], P(('region', 'patch'))
- grad_vectors: float32 [3072], replicated
The draws below stay inside these ranges and needn't reach their ends.
Inputs may be any that keep to these rules, and one draw needn't show every extreme that they name: `send_rows`: list 0 of a patch goes to the patch one index below, list 1 to the one above, cyclically within its region. Live entries are distinct own-node indices and stand first, the rest are -1; each list has half of 32 to 32 live entries, and some list is full. `senders`: below 256 a sender is an own node; 256 + j is the j-th row received from the patch below, 288 + j the j-th from the patch above; only live rows are named.
All inputs are finite; a program needn't handle non-finite values.
Results may differ from the reference program's by a relative error of at most 0.0063.
Values may be sent and summed in bfloat16 or wider, within the bound.
A program may use at most 128 MiB of HBM per device.

```python
import math
import jax
import jax.numpy as jnp
from jax import lax

D = 512
H = 512
NODE_DEV = 256
SEND = 32
EDGE_DEV = 1024
NODES = 65536
EDGES = 262144
N_REGION = 8
N_PATCH = 32


def halo_counts(key):
    counts = jax.random.randint(jax.random.fold_in(key, 11), (N_REGION * N_PATCH, 2), SEND // 2, SEND + 1)
    chosen = jax.random.randint(jax.random.fold_in(key, 12), (), 0, N_REGION * N_PATCH)
    places = jnp.arange(N_REGION * N_PATCH, dtype=jnp.int32)
    counts = jnp.where((places == chosen)[:, None], SEND, counts)
    return counts.reshape(N_REGION, N_PATCH, 2).astype(jnp.int32)


def draw_send_rows(key, part):
    counts = halo_counts(key).reshape(-1)
    list_keys = jax.random.split(jax.random.fold_in(key, 13), N_REGION * N_PATCH * 2)
    chosen = jax.vmap(lambda one_key: jax.random.permutation(one_key, NODE_DEV)[:SEND])(list_keys).astype(jnp.int32)
    slots = jnp.arange(SEND, dtype=jnp.int32)
    filled = jnp.where(slots[None, :] < counts[:, None], chosen, -1)
    return filled.reshape(N_REGION, N_PATCH, 2, SEND).astype(jnp.int32)


def draw_senders(key, part):
    counts = halo_counts(key)
    lower_count = jnp.roll(counts[:, :, 1], 1, axis=1).reshape(-1)
    upper_count = jnp.roll(counts[:, :, 0], -1, axis=1).reshape(-1)
    devices_all = N_REGION * N_PATCH
    shape = (devices_all, EDGE_DEV)
    kinds = jax.random.randint(jax.random.fold_in(key, 21), shape, 0, 10)
    own_pick = jax.random.randint(jax.random.fold_in(key, 22), shape, 0, NODE_DEV)
    lower_pick = NODE_DEV + jax.random.randint(jax.random.fold_in(key, 23), shape, 0, lower_count[:, None])
    upper_pick = NODE_DEV + SEND + jax.random.randint(jax.random.fold_in(key, 24), shape, 0, upper_count[:, None])
    chosen = jnp.where(kinds < 6, own_pick, jnp.where(kinds < 8, lower_pick, upper_pick))
    column = jnp.arange(EDGE_DEV, dtype=jnp.int32)[None, :]
    chosen = jnp.where(column == EDGE_DEV - 1, (NODE_DEV + SEND - 1 + upper_count)[:, None], chosen)
    chosen = jnp.where(column == EDGE_DEV - 2, (NODE_DEV - 1 + lower_count)[:, None], chosen)
    chosen = jnp.where(column == EDGE_DEV - 3, 0, chosen)
    return chosen.reshape(-1).astype(jnp.int32)


def plant(array, own_key, smallest, largest):
    longest = array.shape.index(max(array.shape))
    spots = []
    for shift in (0, 1):
        where = [jax.random.randint(jax.random.fold_in(own_key, axis), (), 0, length) for axis, length in enumerate(array.shape)]
        where[longest] = (where[longest] + shift) % array.shape[longest]
        spots.append(tuple(where))
    return array.at[spots[0]].set(smallest).at[spots[1]].set(largest)


def shard_levels(key, dims, cuts, low, high):
    gain, own = 1.0, jax.random.fold_in(key, 6)
    for axis_at, parts in cuts:
        heights = jnp.exp(jax.random.uniform(jax.random.fold_in(own, axis_at), (parts,), jnp.float32, low / len(cuts), high / len(cuts)))
        gain = gain * jnp.repeat(heights, dims[axis_at] // parts).reshape([-1 if axis == axis_at else 1 for axis in range(len(dims))])
    return gain


def scatter_about(own_key, extent, deviation, limit, shards=(), kind=jnp.bfloat16):
    drawn = deviation * jax.random.normal(own_key, extent, jnp.float32)
    if shards:
        drawn = drawn * shard_levels(own_key, extent, shards, -0.22, 0.18)
    return jnp.clip(drawn, -limit, limit).astype(kind)


def setup_inputs(seed: int = 0) -> dict:
    splits = jax.random.split(jax.random.key(seed), 18)
    nodes = scatter_about(splits[0], (NODES, D), 1.0, 6.0, ((0, 256),))
    edges = scatter_about(splits[1], (EDGES, D), 1.0, 6.0, ((0, 256),))
    node_cotan = scatter_about(splits[2], (NODES, D), 1.0, 6.0, ((0, 256),))
    edge_cotan = scatter_about(splits[3], (EDGES, D), 1.0, 6.0, ((0, 256),))
    edge_inner = scatter_about(splits[4], (3 * D, H), (3 * D) ** -0.5, 0.15625)
    edge_outer = scatter_about(splits[5], (H, D), H ** -0.5, 0.25)
    node_inner = scatter_about(splits[6], (2 * D, H), (2 * D) ** -0.5, 0.1875)
    node_outer = scatter_about(splits[7], (H, D), H ** -0.5, 0.25)
    edge_shift = scatter_about(splits[8], (H,), 1.0, 4.0, (), jnp.float32)
    edge_offset = scatter_about(splits[9], (D,), 1.0, 4.0, (), jnp.float32)
    edge_gain = jnp.clip(jax.random.uniform(splits[10], (D,), jnp.float32, 0.5, 1.5), 0.5, 1.5)
    node_shift = scatter_about(splits[11], (H,), 1.0, 4.0, (), jnp.float32)
    node_offset = scatter_about(splits[12], (D,), 1.0, 4.0, (), jnp.float32)
    node_gain = jnp.clip(jax.random.uniform(splits[13], (D,), jnp.float32, 0.5, 1.5), 0.5, 1.5)
    send_rows = draw_send_rows(jax.random.fold_in(splits[17], 71), 0)
    senders = draw_senders(jax.random.fold_in(splits[17], 71), 0)
    receivers = plant(jax.random.randint(splits[16], (EDGES,), 0, NODE_DEV), jax.random.fold_in(splits[16], 1), 0, NODE_DEV - 1).astype(jnp.int32)
    return dict(nodes=nodes, edges=edges, node_cotan=node_cotan, edge_cotan=edge_cotan, edge_inner=edge_inner, edge_outer=edge_outer, node_inner=node_inner, node_outer=node_outer, edge_shift=edge_shift, edge_offset=edge_offset, edge_gain=edge_gain, node_shift=node_shift, node_offset=node_offset, node_gain=node_gain, send_rows=send_rows, senders=senders, receivers=receivers)


def layer_norm(values):
    centred = values - lax.optimization_barrier(jnp.mean(values, axis=-1, keepdims=True))
    invstd = lax.rsqrt(lax.optimization_barrier(jnp.mean(centred * centred, axis=-1, keepdims=True)) + 1e-05)
    return (centred * invstd, invstd)

def norm_back(upstream, normed, invstd, gains):
    scaled = upstream * gains
    return invstd * (scaled - lax.optimization_barrier(jnp.mean(scaled, axis=-1, keepdims=True)) - normed * lax.optimization_barrier(jnp.mean(scaled * normed, axis=-1, keepdims=True)))

def activation_grad(preact):
    sigmoid_val = jax.nn.sigmoid(preact)
    return sigmoid_val * (1.0 + preact * (1.0 - sigmoid_val))

def contract_rows(left, right):
    return jnp.dot(left.T, right, preferred_element_type=jnp.float32)

def reference(nodes, edges, node_cotan, edge_cotan, edge_inner, edge_outer, node_inner, node_outer, edge_shift, edge_offset, edge_gain, node_shift, node_offset, node_gain, send_rows, senders, receivers):
    devices_all = N_REGION * N_PATCH
    node_blocks = nodes.reshape(devices_all, NODE_DEV, D)
    edge_blocks = edges.reshape(devices_all, EDGE_DEV, D)
    ncotan_blocks = node_cotan.reshape(devices_all, NODE_DEV, D)
    ecotan_blocks = edge_cotan.reshape(devices_all, EDGE_DEV, D)
    send_lists = send_rows.reshape(devices_all, 2 * SEND)
    sender_blocks = senders.reshape(devices_all, EDGE_DEV)
    receiver_blocks = receivers.reshape(devices_all, EDGE_DEV)
    node_ids = jnp.arange(NODE_DEV, dtype=jnp.int32)
    lookup_ids = jnp.arange(NODE_DEV + 2 * SEND, dtype=jnp.int32)
    edge_norm = 1.0 / math.sqrt(EDGES)
    node_norm = 1.0 / math.sqrt(NODES)

    def outgoing_rows(block, lists):
        pick = (lists[:, None] == node_ids[None, :]).astype(jnp.bfloat16)
        return jnp.dot(pick, block, preferred_element_type=jnp.float32).astype(jnp.bfloat16)
    outgoing = jax.vmap(outgoing_rows)(node_blocks, send_lists).reshape(N_REGION, N_PATCH, 2, SEND, D)
    from_lower = jnp.roll(outgoing[:, :, 1], 1, axis=1)
    from_upper = jnp.roll(outgoing[:, :, 0], -1, axis=1)
    received = jnp.concatenate([from_lower, from_upper], axis=2).reshape(devices_all, 2 * SEND, D)

    def local_pass(carry, items):
        flat_sum, vector_sum = carry
        own_nodes, own_edges, ncotan, ecotan, rows_in, sender_ids, receiver_ids = items
        lookup = jnp.concatenate([own_nodes, rows_in], axis=0)
        pick_sender = (sender_ids[:, None] == lookup_ids[None, :]).astype(jnp.bfloat16)
        pick_receiver = (receiver_ids[:, None] == node_ids[None, :]).astype(jnp.bfloat16)
        sender_rows = jnp.dot(pick_sender, lookup, preferred_element_type=jnp.float32).astype(jnp.bfloat16)
        receiver_rows = jnp.dot(pick_receiver, own_nodes, preferred_element_type=jnp.float32).astype(jnp.bfloat16)
        edge_inputs = jnp.concatenate([own_edges, sender_rows, receiver_rows], axis=1)
        edge_preact = jnp.dot(edge_inputs, edge_inner, preferred_element_type=jnp.float32) + edge_shift
        edge_hidden = jax.nn.silu(edge_preact).astype(jnp.bfloat16)
        edge_linear = jnp.dot(edge_hidden, edge_outer, preferred_element_type=jnp.float32) + edge_offset
        edge_normed, edge_invstd = layer_norm(edge_linear)
        edge_fresh = (own_edges.astype(jnp.float32) + edge_gain * edge_normed).astype(jnp.bfloat16)
        aggregate = contract_rows(pick_receiver, edge_fresh).astype(jnp.bfloat16)
        node_inputs = jnp.concatenate([own_nodes, aggregate], axis=1)
        node_preact = jnp.dot(node_inputs, node_inner, preferred_element_type=jnp.float32) + node_shift
        node_hidden = jax.nn.silu(node_preact).astype(jnp.bfloat16)
        node_linear = jnp.dot(node_hidden, node_outer, preferred_element_type=jnp.float32) + node_offset
        node_normed, node_invstd = layer_norm(node_linear)
        cotan_node = ncotan.astype(jnp.float32)
        linear_back = norm_back(cotan_node, node_normed, node_invstd, node_gain)
        linear_half = linear_back.astype(jnp.bfloat16)
        preact_back = jnp.dot(linear_half, node_outer.T, preferred_element_type=jnp.float32) * activation_grad(node_preact)
        preact_half = preact_back.astype(jnp.bfloat16)
        inputs_back = jnp.dot(preact_half, node_inner.T, preferred_element_type=jnp.float32)
        aggregate_half = inputs_back[:, D:].astype(jnp.bfloat16)
        fresh_back = ecotan.astype(jnp.float32) + jnp.dot(pick_receiver, aggregate_half, preferred_element_type=jnp.float32)
        elinear_back = norm_back(fresh_back, edge_normed, edge_invstd, edge_gain)
        elinear_half = elinear_back.astype(jnp.bfloat16)
        epreact_back = jnp.dot(elinear_half, edge_outer.T, preferred_element_type=jnp.float32) * activation_grad(edge_preact)
        epreact_half = epreact_back.astype(jnp.bfloat16)
        einputs_back = jnp.dot(epreact_half, edge_inner.T, preferred_element_type=jnp.float32)
        grad_edge_block = (fresh_back + einputs_back[:, :D]).astype(jnp.bfloat16)
        sender_half = einputs_back[:, D:2 * D].astype(jnp.bfloat16)
        receiver_half = einputs_back[:, 2 * D:].astype(jnp.bfloat16)
        lookup_back = contract_rows(pick_sender, sender_half)
        partial_nodes = cotan_node + inputs_back[:, :D] + lookup_back[:NODE_DEV] + contract_rows(pick_receiver, receiver_half)
        rim_back = lookup_back[NODE_DEV:].reshape(2, SEND, D)
        flat_terms = jnp.concatenate([(contract_rows(edge_inputs, epreact_half) * edge_norm).reshape(-1), (contract_rows(edge_hidden, elinear_half) * edge_norm).reshape(-1), (contract_rows(node_inputs, preact_half) * node_norm).reshape(-1), (contract_rows(node_hidden, linear_half) * node_norm).reshape(-1)])
        vector_terms = jnp.concatenate([lax.optimization_barrier(jnp.sum(epreact_back, axis=0)) * edge_norm, lax.optimization_barrier(jnp.sum(elinear_back, axis=0)) * edge_norm, lax.optimization_barrier(jnp.sum(fresh_back * edge_normed, axis=0)) * edge_norm, lax.optimization_barrier(jnp.sum(preact_back, axis=0)) * node_norm, lax.optimization_barrier(jnp.sum(linear_back, axis=0)) * node_norm, lax.optimization_barrier(jnp.sum(cotan_node * node_normed, axis=0)) * node_norm])
        return ((flat_sum + flat_terms, vector_sum + vector_terms), (partial_nodes, grad_edge_block, rim_back))
    start = (jnp.zeros((7 * D * H,), jnp.float32), jnp.zeros((2 * H + 4 * D,), jnp.float32))
    sums, stacked = lax.scan(local_pass, start, (node_blocks, edge_blocks, ncotan_blocks, ecotan_blocks, received, sender_blocks, receiver_blocks))
    grad_weights, grad_vectors = sums
    partial_nodes, grad_edge_blocks, rim_all = stacked
    rim_all = rim_all.reshape(N_REGION, N_PATCH, 2, SEND, D)
    back_lower = jnp.roll(rim_all[:, :, 1], 1, axis=1)
    back_upper = jnp.roll(rim_all[:, :, 0], -1, axis=1)
    back_rows = jnp.concatenate([back_lower, back_upper], axis=2).reshape(devices_all, 2 * SEND, D)

    def rim_add(lists, rows_back):
        pick = (lists[:, None] == node_ids[None, :]).astype(jnp.float32)
        return jnp.dot(pick.T, rows_back, precision=lax.Precision.HIGHEST, preferred_element_type=jnp.float32)
    from_rims = jax.vmap(rim_add)(send_lists, back_rows)
    grad_nodes = (partial_nodes + from_rims).reshape(NODES, D)
    grad_edges = grad_edge_blocks.reshape(EDGES, D)
    return (grad_nodes, grad_edges, grad_weights, grad_vectors)
```

```python
import math

import jax
import jax.numpy as jnp
from jax import lax
from jax.experimental import pallas as pl
from jax.experimental.pallas import tpu as pltpu
from jax.sharding import PartitionSpec as P

MESH = pl.DeviceIdType.MESH
NX, NC, NY, NZ = 4, 2, 4, 8
WIDTH, HALF = 512, 256
BLOCK, QUARTER, SHARE, PAD = 448, 112, 14, 16


def coordinates():
    region, patch = lax.axis_index("region"), lax.axis_index("patch")
    return region // NC, lax.rem(region, NC), patch // NZ, lax.rem(patch, NZ)


def at(x, c, y, z):
    return (x * NC + c, y * NZ + z)


def peers():
    x, c, y, z = coordinates()
    found = [at(x, 1 - c, y, z)]
    found += [at(lax.rem(x + k, NX), c, y, z) for k in range(1, NX)]
    found += [at(x, c, lax.rem(y + k, NY), z) for k in range(1, NY)]
    found += [at(x, c, y, lax.rem(z + k, NZ)) for k in range(1, NZ)]
    return found


def entry_barrier():
    barrier = pltpu.get_barrier_semaphore()
    found = peers()
    for device in found:
        pl.semaphore_signal(barrier, inc=1, device_id=device, device_id_type=MESH)
    pl.semaphore_wait(barrier, len(found))


def send(src, dst, send_sem, recv_sem, device):
    return pltpu.make_async_remote_copy(
        src_ref=src,
        dst_ref=dst,
        send_sem=send_sem,
        recv_sem=recv_sem,
        device_id=device,
        device_id_type=MESH,
    )


def chunks(total, step, body):
    def one(i, carry):
        body(pl.multiple_of(i * step, step))
        return carry

    lax.fori_loop(0, total // step, one, 0)


def reduce_scratch():
    bf16, f32 = jnp.bfloat16, jnp.float32
    dma = pltpu.SemaphoreType.DMA
    return dict(
        sb=pltpu.VMEM((NX, NC, BLOCK, WIDTH), bf16),
        r0=pltpu.VMEM((NX, BLOCK, WIDTH), bf16),
        b1=pltpu.VMEM((NX, BLOCK, WIDTH), bf16),
        r1x=pltpu.VMEM((NX, BLOCK, HALF), bf16),
        r1y=pltpu.VMEM((NY, NX, QUARTER, HALF), bf16),
        a1x=pltpu.VMEM((NY, QUARTER, HALF), f32),
        b2x=pltpu.VMEM((NY, QUARTER, HALF), bf16),
        r2x=pltpu.VMEM((NY, QUARTER, HALF), bf16),
        a1y=pltpu.VMEM((NX, QUARTER, HALF), f32),
        b2y=pltpu.VMEM((NX, QUARTER, HALF), bf16),
        r2y=pltpu.VMEM((NX, QUARTER, HALF), bf16),
        packed=pltpu.VMEM((NZ, PAD, WIDTH), f32),
        b3=pltpu.VMEM((NZ, PAD, WIDTH), bf16),
        r3=pltpu.VMEM((NZ, PAD, WIDTH), bf16),
        s0=dma((NX,)),
        q0=dma((NX,)),
        s1x=dma((NX,)),
        q1x=dma((NX,)),
        s1y=dma((2, NY)),
        q1y=dma((2, NY)),
        s2x=dma((NY,)),
        q2x=dma((NY,)),
        s2y=dma((NX,)),
        q2y=dma((NX,)),
        s3=dma((NZ,)),
        q3=dma((NZ,)),
        vc=pltpu.VMEM((2, 8, WIDTH), f32),
        vx=pltpu.VMEM((NX, 8, WIDTH), f32),
        vy=pltpu.VMEM((NY, 8, WIDTH), f32),
        vz=pltpu.VMEM((NZ, 8, WIDTH), f32),
        us=dma((1 + NX + NY + NZ,)),
        uq=dma((1 + NX + NY + NZ,)),
    )


class Reducer:
    def __init__(self, g, bufs):
        self.g, self.b = g, bufs
        self.x, self.c, self.y, self.z = coordinates()
        self.piece_xs = ((2, 3), (0, 1))

    def core_copies(self, piece):
        b = self.b
        return [
            send(
                b["sb"].at[xx, 1 - self.c],
                b["r0"].at[xx],
                b["s0"].at[xx],
                b["q0"].at[xx],
                at(self.x, 1 - self.c, self.y, self.z),
            )
            for xx in self.piece_xs[piece]
        ]

    def core_start(self, piece):
        for copy in self.core_copies(piece):
            copy.start()

    def round_blocks(self, piece):
        b, g = self.b, self.g
        for xx in self.piece_xs[piece]:
            for cc in range(NC):

                def body(i, xx=xx, cc=cc):
                    b["sb"][xx, cc, pl.ds(i, 64)] = g[xx, cc, pl.ds(i, 64)].astype(jnp.bfloat16)

                chunks(BLOCK, 64, body)

    def first_x(self, xx):
        b = self.b
        return send(
            b["b1"].at[xx, :, pl.ds(0, HALF)],
            b["r1x"].at[self.x],
            b["s1x"].at[xx],
            b["q1x"].at[self.x],
            at(xx, self.c, self.y, self.z),
        )

    def first_y(self, piece, k):
        b = self.b
        to = lax.rem(self.y + k, NY)
        xa = self.piece_xs[piece][0]
        return send(
            b["b1"].at[pl.ds(xa, 2), pl.ds(pl.multiple_of(to * QUARTER, 16), QUARTER), pl.ds(HALF, HALF)],
            b["r1y"].at[k, pl.ds(xa, 2)],
            b["s1y"].at[piece, k],
            b["q1y"].at[piece, k],
            at(self.x, self.c, to, self.z),
        )

    def first_start(self, piece):
        b, g = self.b, self.g
        for copy in self.core_copies(piece):
            copy.wait_recv()
        for xx in self.piece_xs[piece]:

            def body(i, xx=xx):
                total = g[xx, self.c, pl.ds(i, 64)] + b["r0"][xx, pl.ds(i, 64)].astype(jnp.float32)
                g[xx, self.c, pl.ds(i, 64)] = total
                b["b1"][xx, pl.ds(i, 64)] = total.astype(jnp.bfloat16)

            chunks(BLOCK, 64, body)
        for k in (2, 1, 3):
            self.first_y(piece, k).start()
        for xx in self.piece_xs[piece]:

            @pl.when(self.x != xx)
            def _(xx=xx):
                self.first_x(xx).start()

    def second_x(self, k):
        b = self.b
        to = lax.rem(self.y + k, NY)
        return send(
            b["b2x"].at[to],
            b["r2x"].at[k],
            b["s2x"].at[k],
            b["q2x"].at[k],
            at(self.x, self.c, to, self.z),
        )

    def second_y(self, xx):
        b = self.b
        return send(
            b["b2y"].at[xx],
            b["r2y"].at[self.x],
            b["s2y"].at[xx],
            b["q2y"].at[self.x],
            at(xx, self.c, self.y, self.z),
        )

    def second_y_start(self, piece):
        b, g = self.b, self.g
        for k in (1, 3, 2):
            self.first_y(piece, k).wait_recv()
        base = self.y * QUARTER
        for xx in self.piece_xs[piece]:

            def body(i, xx=xx):
                total = g[xx, self.c, pl.ds(pl.multiple_of(base + i, 16), 16), pl.ds(HALF, HALF)]
                for k in range(1, NY):
                    total += b["r1y"][k, xx, pl.ds(i, 16)].astype(jnp.float32)
                b["a1y"][xx, pl.ds(i, 16)] = total
                b["b2y"][xx, pl.ds(i, 16)] = total.astype(jnp.bfloat16)

            chunks(QUARTER, 16, body)
        for xx in self.piece_xs[piece]:

            @pl.when(self.x != xx)
            def _(xx=xx):
                self.second_y(xx).start()

    def from_x(self, recv, sems, like):
        found = []
        for k in (1, 3, 2):
            source = lax.rem(self.x + k, NX)
            found.append(send(like, recv.at[source], sems[0].at[source], sems[1].at[source], at(source, self.c, self.y, self.z)))
        return found

    def second_x_start(self):
        b, g = self.b, self.g
        for copy in self.from_x(b["r1x"], (b["s1x"], b["q1x"]), b["r1x"].at[0]):
            copy.wait_recv()
        for yy in range(NY):

            def body(i, yy=yy):
                total = g[self.x, self.c, pl.ds(yy * QUARTER + i, 16), pl.ds(0, HALF)]
                for k in range(1, NX):
                    source = lax.rem(self.x + k, NX)
                    total += b["r1x"][source, pl.ds(yy * QUARTER + i, 16)].astype(jnp.float32)
                b["a1x"][yy, pl.ds(i, 16)] = total
                b["b2x"][yy, pl.ds(i, 16)] = total.astype(jnp.bfloat16)

            chunks(QUARTER, 16, body)
        for k in (2, 1, 3):
            self.second_x(k).start()

    def third(self, k):
        b = self.b
        to = lax.rem(self.z + k, NZ)
        return send(
            b["b3"].at[to],
            b["r3"].at[k],
            b["s3"].at[k],
            b["q3"].at[k],
            at(self.x, self.c, self.y, to),
        )

    def third_start(self):
        b = self.b
        for k in range(1, NY):
            self.second_x(k).wait_recv()
        for copy in self.from_x(b["r2y"], (b["s2y"], b["q2y"]), b["r2y"].at[0]):
            copy.wait_recv()
        for i in range(NZ):
            rows = pl.ds(i * SHARE, SHARE)
            left = b["a1x"][self.y, rows]
            right = b["a1y"][self.x, rows]
            for k in range(1, NY):
                left += b["r2x"][k, rows].astype(jnp.float32)
                right += b["r2y"][lax.rem(self.x + k, NX), rows].astype(jnp.float32)
            both = jnp.concatenate([left, right], axis=1)
            b["packed"][i, pl.ds(0, SHARE)] = both
            b["b3"][i, pl.ds(0, SHARE)] = both.astype(jnp.bfloat16)
        for k in (4, 3, 5, 2, 6, 1, 7):
            self.third(k).start()

    def finish(self, out):
        b = self.b
        for k in range(1, NZ):
            self.third(k).wait_recv()
        total = b["packed"][self.z, pl.ds(0, SHARE)]
        for k in range(1, NZ):
            total += b["r3"][k, pl.ds(0, SHARE)].astype(jnp.float32)
        for j in range(WIDTH // 128):
            out[pl.ds(j, SHARE, stride=WIDTH // 128), :] = total[:, 128 * j : 128 * j + 128]

    def drain(self):
        for piece in range(2):
            for copy in self.core_copies(piece):
                copy.wait_send()
            for k in range(1, NY):
                self.first_y(piece, k).wait_send()
        for xx in range(NX):

            @pl.when(self.x != xx)
            def _(xx=xx):
                self.first_x(xx).wait_send()
                self.second_y(xx).wait_send()

        for k in range(1, NY):
            self.second_x(k).wait_send()
        for k in range(1, NZ):
            self.third(k).wait_send()

    def vector_copies(self, stage):
        b = self.b
        x, c, y, z = self.x, self.c, self.y, self.z
        if stage == 0:
            return [send(b["vc"].at[0], b["vc"].at[1], b["us"].at[0], b["uq"].at[0], at(x, 1 - c, y, z))]
        buf, base, count, me = (
            (b["vx"], 1, NX, x),
            (b["vy"], 1 + NX, NY, y),
            (b["vz"], 1 + NX + NY, NZ, z),
        )[stage - 1]
        found = []
        for k in range(1, count):
            to = lax.rem(me + k, count)
            device = (at(to, c, y, z), at(x, c, to, z), at(x, c, y, to))[stage - 1]
            found.append((k, to, device, buf, base, me, count))
        return [
            send(buf.at[me], buf.at[me], b["us"].at[base + k], b["uq"].at[base + k], device)
            for k, to, device, buf, base, me, count in found
        ]

    def vector_start(self, stage, value):
        b = self.b
        if stage == 0:
            b["vc"][0] = value
        else:
            (b["vx"], b["vy"], b["vz"])[stage - 1][(self.x, self.y, self.z)[stage - 1]] = value
        for copy in self.vector_copies(stage):
            copy.start()

    def vector_value(self, stage):
        b = self.b
        for copy in self.vector_copies(stage):
            copy.wait_recv()
        if stage == 0:
            return b["vc"][0] + b["vc"][1]
        buf = (b["vx"], b["vy"], b["vz"])[stage - 1]
        total = buf[0]
        for i in range(1, buf.shape[0]):
            total += buf[i]
        return total

    def vector_drain(self):
        for stage in range(4):
            for copy in self.vector_copies(stage):
                copy.wait_send()


def reduce_all(inner_e, outer_e, inner_n, outer_n, vectors):
    names = list(reduce_scratch())
    sources = (inner_e, outer_e, inner_n, outer_n)

    def kernel(e_in, e_out, n_in, n_out, vec, out, vec_out, g, load, *rest):
        bufs = dict(zip(names, rest))
        flat = g.reshape(NX * NC * BLOCK, WIDTH)
        copies, row = [], 0
        for i, ref in enumerate((e_in, e_out, n_in, n_out)):
            rows = ref.shape[0]
            copies.append(pltpu.make_async_copy(ref, flat.at[pl.ds(row, rows)], load.at[i]))
            row += rows
        for copy in copies:
            copy.start()
        entry_barrier()
        red = Reducer(g, bufs)
        red.vector_start(0, vec[...])
        for copy in copies:
            copy.wait()
        for piece in range(2):
            red.round_blocks(piece)
            red.core_start(piece)
        red.vector_start(1, red.vector_value(0))
        for piece in range(2):
            red.first_start(piece)
        red.vector_start(2, red.vector_value(1))
        for piece in range(2):
            red.second_y_start(piece)
        red.second_x_start()
        red.vector_start(3, red.vector_value(2))
        red.third_start()
        vec_out[...] = red.vector_value(3)
        red.finish(out)
        red.drain()
        red.vector_drain()

    any_spec = pl.BlockSpec(memory_space=pl.ANY)
    vmem_spec = pl.BlockSpec(memory_space=pltpu.VMEM)
    return pl.pallas_call(
        kernel,
        out_shape=(
            jax.ShapeDtypeStruct((SHARE * WIDTH // 128, 128), jnp.float32),
            jax.ShapeDtypeStruct((8, WIDTH), jnp.float32),
        ),
        in_specs=[any_spec] * 4 + [vmem_spec],
        out_specs=(vmem_spec, vmem_spec),
        scratch_shapes=[
            pltpu.VMEM((NX, NC, BLOCK, WIDTH), jnp.float32),
            pltpu.SemaphoreType.DMA((4,)),
            *reduce_scratch().values(),
        ],
        compiler_params=pltpu.CompilerParams(
            collective_id=0, has_side_effects=True, vmem_limit_bytes=48 * 1024 * 1024
        ),
        name="reduce_weights",
    )(*sources, vectors)


def extended(block, sides, width):
    for axis, dim in sides:
        count = lax.axis_size(axis)
        forward = [(i, i + 1) for i in range(count - 1)]
        forward.append((count - 1, 0))
        backward = [(target, source) for source, target in forward]
        low = lax.ppermute(
            lax.slice_in_dim(block, block.shape[dim] - width, None, axis=dim), axis, forward
        )
        high = lax.ppermute(lax.slice_in_dim(block, 0, width, axis=dim), axis, backward)
        block = jnp.concatenate([low, block, high], axis=dim)
    return block


def layer_norm(values):
    centred = values - jnp.mean(values, axis=-1, keepdims=True)
    invstd = lax.rsqrt(jnp.mean(centred * centred, axis=-1, keepdims=True) + 1e-05)
    return (centred * invstd, invstd)


def norm_back(upstream, normed, invstd, gains):
    scaled = upstream * gains
    return invstd * (
        scaled
        - jnp.mean(scaled, axis=-1, keepdims=True)
        - normed * jnp.mean(scaled * normed, axis=-1, keepdims=True)
    )


def activation_grad(preact):
    sigmoid_val = jax.nn.sigmoid(preact)
    return sigmoid_val * (1.0 + preact * (1.0 - sigmoid_val))


def contract_rows(left, right):
    return lax.dot_general(
        left, right, (((0,), (0,)), ((), ())), preferred_element_type=jnp.float32
    )


def per_device(
    nodes,
    edges,
    node_cotan,
    edge_cotan,
    edge_inner,
    edge_outer,
    node_inner,
    node_outer,
    edge_shift,
    edge_offset,
    edge_gain,
    node_shift,
    node_offset,
    node_gain,
    send_rows,
    senders,
    receivers,
):
    node_count = nodes.shape[0]
    edge_count = edges.shape[0]
    feature_width = nodes.shape[1]
    send_lists = send_rows.reshape(-1)
    slot_count = send_lists.shape[0] // 2
    devices_all = lax.axis_size("region") * lax.axis_size("patch")
    edge_norm = 1.0 / math.sqrt(edge_count * devices_all)
    node_norm = 1.0 / math.sqrt(node_count * devices_all)
    node_ids = jnp.arange(node_count, dtype=jnp.int32)
    pick_send = (send_lists[:, None] == node_ids[None, :]).astype(jnp.bfloat16)
    outgoing = jnp.dot(pick_send, nodes, preferred_element_type=jnp.float32).astype(jnp.bfloat16)
    received = extended(outgoing.reshape(2, slot_count, feature_width), (("patch", 0),), 1)
    lookup = jnp.concatenate([nodes, received[0], received[3]], axis=0)
    lookup_ids = jnp.arange(lookup.shape[0], dtype=jnp.int32)
    pick_sender = (senders[:, None] == lookup_ids[None, :]).astype(jnp.bfloat16)
    pick_receiver = (receivers[:, None] == node_ids[None, :]).astype(jnp.bfloat16)
    sender_rows = jnp.dot(pick_sender, lookup, preferred_element_type=jnp.float32).astype(
        jnp.bfloat16
    )
    receiver_rows = jnp.dot(pick_receiver, nodes, preferred_element_type=jnp.float32).astype(
        jnp.bfloat16
    )
    edge_inputs = jnp.concatenate([edges, sender_rows, receiver_rows], axis=1)
    edge_preact = jnp.dot(edge_inputs, edge_inner, preferred_element_type=jnp.float32) + edge_shift
    edge_hidden = jax.nn.silu(edge_preact).astype(jnp.bfloat16)
    edge_linear = jnp.dot(edge_hidden, edge_outer, preferred_element_type=jnp.float32) + edge_offset
    edge_normed, edge_invstd = layer_norm(edge_linear)
    edge_fresh = (edges.astype(jnp.float32) + edge_gain * edge_normed).astype(jnp.bfloat16)
    aggregate = contract_rows(pick_receiver, edge_fresh).astype(jnp.bfloat16)
    node_inputs = jnp.concatenate([nodes, aggregate], axis=1)
    node_preact = jnp.dot(node_inputs, node_inner, preferred_element_type=jnp.float32) + node_shift
    node_hidden = jax.nn.silu(node_preact).astype(jnp.bfloat16)
    node_linear = jnp.dot(node_hidden, node_outer, preferred_element_type=jnp.float32) + node_offset
    node_normed, node_invstd = layer_norm(node_linear)
    cotan_node = node_cotan.astype(jnp.float32)
    linear_back = norm_back(cotan_node, node_normed, node_invstd, node_gain)
    linear_half = linear_back.astype(jnp.bfloat16)
    preact_back = jnp.dot(
        linear_half, node_outer.T, preferred_element_type=jnp.float32
    ) * activation_grad(node_preact)
    preact_half = preact_back.astype(jnp.bfloat16)
    inputs_back = jnp.dot(preact_half, node_inner.T, preferred_element_type=jnp.float32)
    aggregate_half = inputs_back[:, feature_width:].astype(jnp.bfloat16)
    fresh_back = edge_cotan.astype(jnp.float32) + jnp.dot(
        pick_receiver, aggregate_half, preferred_element_type=jnp.float32
    )
    elinear_back = norm_back(fresh_back, edge_normed, edge_invstd, edge_gain)
    elinear_half = elinear_back.astype(jnp.bfloat16)
    epreact_back = jnp.dot(
        elinear_half, edge_outer.T, preferred_element_type=jnp.float32
    ) * activation_grad(edge_preact)
    epreact_half = epreact_back.astype(jnp.bfloat16)
    einputs_back = jnp.dot(epreact_half, edge_inner.T, preferred_element_type=jnp.float32)
    grad_edges = (fresh_back + einputs_back[:, :feature_width]).astype(jnp.bfloat16)
    sender_half = einputs_back[:, feature_width : 2 * feature_width].astype(jnp.bfloat16)
    receiver_half = einputs_back[:, 2 * feature_width :].astype(jnp.bfloat16)
    lookup_back = contract_rows(pick_sender, sender_half)
    rim_back = lookup_back[node_count:].reshape(2, slot_count, feature_width)
    returned = extended(rim_back.astype(jnp.bfloat16), (("patch", 0),), 1).astype(rim_back.dtype)
    back_rows = jnp.concatenate([returned[0], returned[3]], axis=0)
    from_rims = lax.dot_general(
        pick_send.astype(jnp.float32),
        back_rows,
        (((0,), (0,)), ((), ())),
        precision=lax.Precision.HIGHEST,
        preferred_element_type=jnp.float32,
    )
    grad_nodes = (
        cotan_node
        + inputs_back[:, :feature_width]
        + lookup_back[:node_count]
        + contract_rows(pick_receiver, receiver_half)
        + from_rims
    )
    vector_terms = jnp.stack(
        [
            jnp.sum(epreact_back, axis=0) * edge_norm,
            jnp.sum(elinear_back, axis=0) * edge_norm,
            jnp.sum(fresh_back * edge_normed, axis=0) * edge_norm,
            jnp.sum(preact_back, axis=0) * node_norm,
            jnp.sum(linear_back, axis=0) * node_norm,
            jnp.sum(cotan_node * node_normed, axis=0) * node_norm,
        ]
    )
    vectors = jnp.concatenate([vector_terms, jnp.zeros((2, feature_width), jnp.float32)], axis=0)
    weights, vector_sums = reduce_all(
        contract_rows(edge_inputs, epreact_half) * edge_norm,
        contract_rows(edge_hidden, elinear_half) * edge_norm,
        contract_rows(node_inputs, preact_half) * node_norm,
        contract_rows(node_hidden, linear_half) * node_norm,
        vectors,
    )
    grad_weights = weights.reshape(-1)
    grad_vectors = vector_sums[:6].reshape(-1)
    return (grad_nodes, grad_edges, grad_weights, grad_vectors)


def solution(mesh):
    in_specs = (
        P(("region", "patch"), None),
        P(("region", "patch"), None),
        P(("region", "patch"), None),
        P(("region", "patch"), None),
        P(),
        P(),
        P(),
        P(),
        P(),
        P(),
        P(),
        P(),
        P(),
        P(),
        P("region", "patch", None, None),
        P(("region", "patch")),
        P(("region", "patch")),
    )
    out_specs = (
        P(("region", "patch"), None),
        P(("region", "patch"), None),
        P(("region", "patch")),
        P(),
    )
    return jax.shard_map(
        per_device, mesh=mesh, in_specs=in_specs, out_specs=out_specs, check_vma=False
    )
```

```python
import math
from types import SimpleNamespace

import jax
import jax.numpy as jnp
from jax import lax
from jax.experimental import pallas as pl
from jax.experimental.pallas import tpu as pltpu
from jax.sharding import PartitionSpec as P

MESH = pl.DeviceIdType.MESH
NX, NC, NY, NZ = 4, 2, 4, 8
WIDTH, HALF = 512, 256
BLOCK, QUARTER, SHARE, PAD = 448, 112, 14, 16


def coordinates():
    region, patch = lax.axis_index("region"), lax.axis_index("patch")
    return region // NC, lax.rem(region, NC), patch // NZ, lax.rem(patch, NZ)


def at(x, c, y, z):
    return (x * NC + c, y * NZ + z)


def beside(step):
    region, patch = lax.axis_index("region"), lax.axis_index("patch")
    return (region, lax.rem(patch + step + NY * NZ, NY * NZ))


def peers():
    x, c, y, z = coordinates()
    found = [at(x, 1 - c, y, z), beside(1), beside(-1)]
    found += [at(lax.rem(x + k, NX), c, y, z) for k in range(1, NX)]
    found += [at(x, c, lax.rem(y + k, NY), z) for k in range(1, NY)]
    found += [at(x, c, y, lax.rem(z + k, NZ)) for k in range(1, NZ)]
    return found


def barrier_signal():
    barrier = pltpu.get_barrier_semaphore()
    for device in peers():
        pl.semaphore_signal(barrier, inc=1, device_id=device, device_id_type=MESH)


def barrier_wait():
    pl.semaphore_wait(pltpu.get_barrier_semaphore(), len(peers()))


def send(src, dst, send_sem, recv_sem, device):
    return pltpu.make_async_remote_copy(
        src_ref=src,
        dst_ref=dst,
        send_sem=send_sem,
        recv_sem=recv_sem,
        device_id=device,
        device_id_type=MESH,
    )


def chunks(total, step, body):
    def one(i, carry):
        body(pl.multiple_of(i * step, step))
        return carry

    lax.fori_loop(0, total // step, one, 0)


def reduce_scratch():
    bf16, f32 = jnp.bfloat16, jnp.float32
    dma = pltpu.SemaphoreType.DMA
    return dict(
        sb=pltpu.VMEM((NX, NC, BLOCK, WIDTH), bf16),
        r0=pltpu.VMEM((NX, BLOCK, WIDTH), bf16),
        b1=pltpu.VMEM((NX, BLOCK, WIDTH), bf16),
        r1x=pltpu.VMEM((NX, BLOCK, HALF), bf16),
        r1y=pltpu.VMEM((NY, NX, QUARTER, HALF), bf16),
        a1x=pltpu.VMEM((NY, QUARTER, HALF), f32),
        b2x=pltpu.VMEM((NY, QUARTER, HALF), bf16),
        r2x=pltpu.VMEM((NY, QUARTER, HALF), bf16),
        a1y=pltpu.VMEM((NX, QUARTER, HALF), f32),
        b2y=pltpu.VMEM((NX, QUARTER, HALF), bf16),
        r2y=pltpu.VMEM((NX, QUARTER, HALF), bf16),
        packed=pltpu.VMEM((NZ, PAD, WIDTH), f32),
        b3=pltpu.VMEM((NZ, PAD, WIDTH), bf16),
        r3=pltpu.VMEM((NZ, PAD, WIDTH), bf16),
        s0=dma((NX,)),
        q0=dma((NX,)),
        s1x=dma((NX,)),
        q1x=dma((NX,)),
        s1y=dma((3, NY)),
        q1y=dma((3, NY)),
        s2x=dma((NY,)),
        q2x=dma((NY,)),
        s2y=dma((NX,)),
        q2y=dma((NX,)),
        s3=dma((NZ,)),
        q3=dma((NZ,)),
        vc=pltpu.VMEM((2, 8, WIDTH), f32),
        vx=pltpu.VMEM((NX, 8, WIDTH), f32),
        vy=pltpu.VMEM((NY, 8, WIDTH), f32),
        vz=pltpu.VMEM((NZ, 8, WIDTH), f32),
        us=dma((1 + NX + NY + NZ,)),
        uq=dma((1 + NX + NY + NZ,)),
    )


class Reducer:
    def __init__(self, g, bufs):
        self.g, self.b = g, bufs
        self.x, self.c, self.y, self.z = coordinates()
        self.piece_xs = ((3,), (2,), (0, 1))

    def core_copies(self, piece):
        b = self.b
        return [
            send(
                b.sb.at[xx, 1 - self.c],
                b.r0.at[xx],
                b.s0.at[xx],
                b.q0.at[xx],
                at(self.x, 1 - self.c, self.y, self.z),
            )
            for xx in self.piece_xs[piece]
        ]

    def core_start(self, piece):
        for copy in self.core_copies(piece):
            copy.start()

    def round_blocks(self, piece):
        b, g = self.b, self.g
        for xx in self.piece_xs[piece]:
            for cc in range(NC):

                def body(i, xx=xx, cc=cc):
                    b.sb[xx, cc, pl.ds(i, 64)] = g[xx, cc, pl.ds(i, 64)].astype(jnp.bfloat16)

                chunks(BLOCK, 64, body)

    def first_x(self, xx):
        b = self.b
        return send(
            b.b1.at[xx, :, pl.ds(0, HALF)],
            b.r1x.at[self.x],
            b.s1x.at[xx],
            b.q1x.at[self.x],
            at(xx, self.c, self.y, self.z),
        )

    def first_y(self, piece, k):
        b = self.b
        to = lax.rem(self.y + k, NY)
        xs = self.piece_xs[piece]
        blocks = pl.ds(xs[0], len(xs))
        return send(
            b.b1.at[blocks, pl.ds(pl.multiple_of(to * QUARTER, 16), QUARTER), pl.ds(HALF, HALF)],
            b.r1y.at[k, blocks],
            b.s1y.at[piece, k],
            b.q1y.at[piece, k],
            at(self.x, self.c, to, self.z),
        )

    def first_start(self, piece):
        b, g = self.b, self.g
        for copy in self.core_copies(piece):
            copy.wait_recv()
        for xx in self.piece_xs[piece]:

            def body(i, xx=xx):
                total = g[xx, self.c, pl.ds(i, 64)] + b.r0[xx, pl.ds(i, 64)].astype(jnp.float32)
                g[xx, self.c, pl.ds(i, 64)] = total
                b.b1[xx, pl.ds(i, 64)] = total.astype(jnp.bfloat16)

            chunks(BLOCK, 64, body)
        for k in (2, 1, 3):
            self.first_y(piece, k).start()
        for xx in self.piece_xs[piece]:

            @pl.when(self.x != xx)
            def _(xx=xx):
                self.first_x(xx).start()

    def second_x(self, k):
        b = self.b
        to = lax.rem(self.y + k, NY)
        return send(
            b.b2x.at[to],
            b.r2x.at[k],
            b.s2x.at[k],
            b.q2x.at[k],
            at(self.x, self.c, to, self.z),
        )

    def second_y(self, xx):
        b = self.b
        return send(
            b.b2y.at[xx],
            b.r2y.at[self.x],
            b.s2y.at[xx],
            b.q2y.at[self.x],
            at(xx, self.c, self.y, self.z),
        )

    def second_y_start(self, piece):
        b, g = self.b, self.g
        for k in (1, 3, 2):
            self.first_y(piece, k).wait_recv()
        base = self.y * QUARTER
        for xx in self.piece_xs[piece]:

            def body(i, xx=xx):
                total = g[xx, self.c, pl.ds(pl.multiple_of(base + i, 16), 16), pl.ds(HALF, HALF)]
                for k in range(1, NY):
                    total += b.r1y[k, xx, pl.ds(i, 16)].astype(jnp.float32)
                b.a1y[xx, pl.ds(i, 16)] = total
                b.b2y[xx, pl.ds(i, 16)] = total.astype(jnp.bfloat16)

            chunks(QUARTER, 16, body)
        for xx in self.piece_xs[piece]:

            @pl.when(self.x != xx)
            def _(xx=xx):
                self.second_y(xx).start()

    def from_x(self, recv, sems, like):
        found = []
        for k in (1, 3, 2):
            source = lax.rem(self.x + k, NX)
            found.append(send(like, recv.at[source], sems[0].at[source], sems[1].at[source], at(source, self.c, self.y, self.z)))
        return found

    def second_x_start(self):
        b, g = self.b, self.g
        for copy in self.from_x(b.r1x, (b.s1x, b.q1x), b.r1x.at[0]):
            copy.wait_recv()
        for yy in range(NY):

            def body(i, yy=yy):
                total = g[self.x, self.c, pl.ds(yy * QUARTER + i, 16), pl.ds(0, HALF)]
                for k in range(1, NX):
                    source = lax.rem(self.x + k, NX)
                    total += b.r1x[source, pl.ds(yy * QUARTER + i, 16)].astype(jnp.float32)
                b.a1x[yy, pl.ds(i, 16)] = total
                b.b2x[yy, pl.ds(i, 16)] = total.astype(jnp.bfloat16)

            chunks(QUARTER, 16, body)
        for k in (2, 1, 3):
            self.second_x(k).start()

    def third(self, k):
        b = self.b
        to = lax.rem(self.z + k, NZ)
        return send(
            b.b3.at[to],
            b.r3.at[k],
            b.s3.at[k],
            b.q3.at[k],
            at(self.x, self.c, self.y, to),
        )

    def third_start(self):
        b = self.b
        for k in range(1, NY):
            self.second_x(k).wait_recv()
        for copy in self.from_x(b.r2y, (b.s2y, b.q2y), b.r2y.at[0]):
            copy.wait_recv()
        for i in range(NZ):
            rows = pl.ds(i * SHARE, SHARE)
            left = b.a1x[self.y, rows]
            right = b.a1y[self.x, rows]
            for k in range(1, NY):
                left += b.r2x[k, rows].astype(jnp.float32)
                right += b.r2y[lax.rem(self.x + k, NX), rows].astype(jnp.float32)
            both = jnp.concatenate([left, right], axis=1)
            b.packed[i, pl.ds(0, SHARE)] = both
            b.b3[i, pl.ds(0, SHARE)] = both.astype(jnp.bfloat16)
        for k in (4, 3, 5, 2, 6, 1, 7):
            self.third(k).start()

    def finish(self, out):
        b = self.b
        for k in range(1, NZ):
            self.third(k).wait_recv()
        total = b.packed[self.z, pl.ds(0, SHARE)]
        for k in range(1, NZ):
            total += b.r3[k, pl.ds(0, SHARE)].astype(jnp.float32)
        for j in range(WIDTH // 128):
            out[pl.ds(j, SHARE, stride=WIDTH // 128), :] = total[:, 128 * j : 128 * j + 128]

    def drain(self):
        for piece in range(len(self.piece_xs)):
            for copy in self.core_copies(piece):
                copy.wait_send()
            for k in range(1, NY):
                self.first_y(piece, k).wait_send()
        for xx in range(NX):

            @pl.when(self.x != xx)
            def _(xx=xx):
                self.first_x(xx).wait_send()
                self.second_y(xx).wait_send()

        for k in range(1, NY):
            self.second_x(k).wait_send()
        for k in range(1, NZ):
            self.third(k).wait_send()

    def vector_copies(self, stage):
        b = self.b
        x, c, y, z = self.x, self.c, self.y, self.z
        if stage == 0:
            return [send(b.vc.at[0], b.vc.at[1], b.us.at[0], b.uq.at[0], at(x, 1 - c, y, z))]
        buf, base, count, me = (
            (b.vx, 1, NX, x),
            (b.vy, 1 + NX, NY, y),
            (b.vz, 1 + NX + NY, NZ, z),
        )[stage - 1]
        found = []
        for k in range(1, count):
            to = lax.rem(me + k, count)
            device = (at(to, c, y, z), at(x, c, to, z), at(x, c, y, to))[stage - 1]
            found.append((k, to, device, buf, base, me, count))
        return [
            send(buf.at[me], buf.at[me], b.us.at[base + k], b.uq.at[base + k], device)
            for k, to, device, buf, base, me, count in found
        ]

    def vector_start(self, stage, value=None):
        b = self.b
        if stage > 0:
            (b.vx, b.vy, b.vz)[stage - 1][(self.x, self.y, self.z)[stage - 1]] = value
        for copy in self.vector_copies(stage):
            copy.start()

    def vector_value(self, stage):
        b = self.b
        for copy in self.vector_copies(stage):
            copy.wait_recv()
        if stage == 0:
            return b.vc[0] + b.vc[1]
        buf = (b.vx, b.vy, b.vz)[stage - 1]
        total = buf[0]
        for i in range(1, buf.shape[0]):
            total += buf[i]
        return total

    def vector_drain(self):
        for stage in range(4):
            for copy in self.vector_copies(stage):
                copy.wait_send()


NODES, EDGES, SLOTS, LOOKUP, PICKS = 256, 1024, 32, 320, 640
TILE = 512


def dot(left, right):
    return jnp.dot(left, right, preferred_element_type=jnp.float32)


def dot_nt(left, right):
    return lax.dot_general(left, right, (((1,), (1,)), ((), ())), preferred_element_type=jnp.float32)


def dot_tn(left, right):
    return lax.dot_general(left, right, (((0,), (0,)), ((), ())), preferred_element_type=jnp.float32)


def layer_norm(values):
    centred = values - jnp.mean(values, axis=-1, keepdims=True)
    invstd = lax.rsqrt(jnp.mean(centred * centred, axis=-1, keepdims=True) + 1e-05)
    return centred * invstd, invstd


def norm_back(upstream, normed, invstd, gains):
    scaled = upstream * gains
    return invstd * (
        scaled
        - jnp.mean(scaled, axis=-1, keepdims=True)
        - normed * jnp.mean(scaled * normed, axis=-1, keepdims=True)
    )


def silu_parts(preact):
    sigmoid = 1.0 / (1.0 + jnp.exp(-preact))
    return preact * sigmoid, sigmoid * (1.0 + preact * (1.0 - sigmoid))


def column_sums(values):
    return jnp.sum(values.reshape(-1, 8, WIDTH), axis=0)


def operands_named(
    nodes, edges, ncot, ecot, wei, weo, wni, wno, eshift, eoff, egain, nshift, noff, ngain, sendid, sndid, rcvid
):
    return SimpleNamespace(**locals())


SMALL = ("eshift", "eoff", "egain", "nshift", "noff", "ngain", "sendid", "sndid", "rcvid")


def compute_scratch():
    bf16, f32 = jnp.bfloat16, jnp.float32
    vm, dma = pltpu.VMEM, pltpu.SemaphoreType.DMA
    return dict(
        g=vm((NX, NC, BLOCK, WIDTH), f32),
        look=vm((LOOKUP, WIDTH), bf16),
        edges_v=vm((EDGES, WIDTH), bf16),
        ncot_v=vm((NODES, WIDTH), bf16),
        ecot_v=vm((EDGES, WIDTH), bf16),
        wei_v=vm((3 * WIDTH, WIDTH), bf16),
        weo_v=vm((WIDTH, WIDTH), bf16),
        wni_v=vm((2 * WIDTH, WIDTH), bf16),
        wno_v=vm((WIDTH, WIDTH), bf16),
        eshift_v=vm((1, WIDTH), f32),
        eoff_v=vm((1, WIDTH), f32),
        egain_v=vm((1, WIDTH), f32),
        nshift_v=vm((1, WIDTH), f32),
        noff_v=vm((1, WIDTH), f32),
        ngain_v=vm((1, WIDTH), f32),
        sendid_v=vm((2, SLOTS), jnp.int32),
        sndid_v=vm((EDGES // 128, 128), jnp.int32),
        rcvid_v=vm((EDGES // 128, 128), jnp.int32),
        loads=dma((18,)),
        pick=vm((EDGES, PICKS), bf16),
        pick_t=vm((PICKS, EDGES), bf16),
        proj=vm((PICKS, WIDTH), bf16),
        outgoing=vm((2 * SLOTS, WIDTH), bf16),
        pre=vm((EDGES, WIDTH), f32),
        dact=vm((EDGES, WIDTH), f32),
        hidden=vm((EDGES, WIDTH), bf16),
        normed=vm((EDGES, WIDTH), f32),
        invstd=vm((EDGES, 128), f32),
        agg=vm((NODES, WIDTH), f32),
        agg_b=vm((NODES, WIDTH), bf16),
        back_b=vm((NODES, WIDTH), bf16),
        nhid=vm((NODES, WIDTH), bf16),
        lhalf=vm((NODES, WIDTH), bf16),
        phalf=vm((NODES, WIDTH), bf16),
        elhalf=vm((EDGES, WIDTH), bf16),
        ephalf=vm((EDGES, WIDTH), bf16),
        gathered=vm((PICKS, WIDTH), bf16),
        rim=vm((2 * SLOTS, WIDTH), bf16),
        back=vm((2 * SLOTS, WIDTH), bf16),
        gnodes=vm((NODES, WIDTH), f32),
        sums=vm((3, 8, WIDTH), f32),
        hs=dma((4,)),
        hq=dma((4,)),
    )


def layer(edge_norm, node_norm, *operands):
    names = list(compute_scratch())
    comm_names = list(reduce_scratch())

    def kernel(*refs):
        given = operands_named(*refs[:17])
        gn_out, ge_out, w_out, v_out = refs[17:21]
        s = SimpleNamespace(**dict(zip(names, refs[21 : 21 + len(names)])))
        bufs = SimpleNamespace(**dict(zip(comm_names, refs[21 + len(names) :])))
        bf16, f32 = jnp.bfloat16, jnp.float32
        barrier_signal()
        red = Reducer(s.g, bufs)
        flat = s.g.reshape(NX * NC * BLOCK, WIDTH)
        wei = given.wei
        loads = dict(
            ecot=(given.ecot, s.ecot_v),
            ncot=(given.ncot, s.ncot_v),
            wno=(given.wno, s.wno_v),
            wni=(given.wni, s.wni_v),
            weo=(given.weo, s.weo_v),
            ws=(wei.at[pl.ds(WIDTH, 2 * WIDTH)], s.wei_v.at[pl.ds(WIDTH, 2 * WIDTH)]),
            edges=(given.edges, s.edges_v),
            we=(wei.at[pl.ds(0, WIDTH)], s.wei_v.at[pl.ds(0, WIDTH)]),
            nodes=(given.nodes, s.look.at[pl.ds(0, NODES)]),
        )
        for name in SMALL:
            loads[name] = (getattr(given, name), getattr(s, name + "_v"))
            setattr(given, name, getattr(s, name + "_v"))
        load = {}
        for i, (name, (src, dst)) in enumerate(reversed(loads.items())):
            load[name] = pltpu.make_async_copy(src, dst, s.loads.at[i])
            load[name].start()
        load = SimpleNamespace(**load)
        w_e = s.wei_v.at[pl.ds(0, WIDTH)]
        w_s = s.wei_v.at[pl.ds(WIDTH, WIDTH)]
        w_r = s.wei_v.at[pl.ds(2 * WIDTH, WIDTH)]
        w_n1 = s.wni_v.at[pl.ds(0, WIDTH)]
        w_n2 = s.wni_v.at[pl.ds(WIDTH, WIDTH)]
        own = s.look.at[pl.ds(0, NODES)]

        for name in SMALL:
            getattr(load, name).wait()

        def one(mask):
            return jnp.where(mask, 1.0, 0.0).astype(bf16)

        send_ids = jnp.concatenate([given.sendid[0:1, :], given.sendid[1:2, :]], axis=1)
        send_t = one(lax.broadcasted_iota(jnp.int32, (NODES, 2 * SLOTS), 0) == send_ids)
        for j in range(EDGES // 128):
            lanes = pl.ds(128 * j, 128)
            snd, rcv = given.sndid[j : j + 1, :], given.rcvid[j : j + 1, :]
            s.pick_t[pl.ds(0, NODES), lanes] = one(lax.broadcasted_iota(jnp.int32, (NODES, 128), 0) == rcv)
            s.pick_t[pl.ds(NODES, PICKS - NODES), lanes] = one(
                lax.broadcasted_iota(jnp.int32, (PICKS - NODES, 128), 0) == snd
            )
            snd_c = jnp.broadcast_to(snd, (128, 128)).T
            rcv_c = jnp.broadcast_to(rcv, (128, 128)).T
            lane = lax.broadcasted_iota(jnp.int32, (128, 128), 1)
            for i in range(2):
                s.pick[pl.ds(128 * j, 128), pl.ds(128 * i, 128)] = one(rcv_c == lane + 128 * i)
            for i in range(3):
                s.pick[pl.ds(128 * j, 128), pl.ds(NODES + 128 * i, 128)] = one(snd_c == lane + 128 * i)
        s.proj[pl.ds(NODES + LOOKUP, 64)] = jnp.zeros((64, WIDTH), bf16)

        load.nodes.wait()
        s.outgoing[...] = dot_tn(send_t, own[...]).astype(bf16)
        halo = [
            send(s.outgoing.at[pl.ds(0, SLOTS)], s.look.at[pl.ds(NODES + SLOTS, SLOTS)], s.hs.at[0], s.hq.at[0], beside(-1)),
            send(s.outgoing.at[pl.ds(SLOTS, SLOTS)], s.look.at[pl.ds(NODES, SLOTS)], s.hs.at[1], s.hq.at[1], beside(1)),
        ]
        barrier_wait()
        for copy in halo:
            copy.start()

        def tiles(body):
            chunks(EDGES, TILE, body)

        load.we.wait()
        load.edges.wait()

        def first(i):
            rows = pl.ds(i, TILE)
            s.pre[rows] = dot(s.edges_v[rows], w_e[...]) + given.eshift[...]

        tiles(first)
        load.ws.wait()
        s.proj[pl.ds(0, NODES)] = dot(own[...], w_r[...]).astype(bf16)
        for copy in halo:
            copy.wait_recv()
        s.proj[pl.ds(NODES, LOOKUP)] = dot(s.look[...], w_s[...]).astype(bf16)
        load.weo.wait()
        s.agg[...] = jnp.zeros((NODES, WIDTH), f32)

        def forward(i):
            rows = pl.ds(i, TILE)
            preact = s.pre[rows] + dot(s.pick[rows], s.proj[...])
            hidden, dact = silu_parts(preact)
            s.dact[rows] = dact
            hidden = hidden.astype(bf16)
            s.hidden[rows] = hidden
            linear = dot(hidden, s.weo_v[...]) + given.eoff[...]
            normed, invstd = layer_norm(linear)
            s.normed[rows] = normed
            s.invstd[rows] = jnp.broadcast_to(invstd, (TILE, 128))
            fresh = (s.edges_v[rows].astype(f32) + given.egain[...] * normed).astype(bf16)
            s.agg[...] += dot(s.pick_t[pl.ds(0, NODES), pl.ds(i, TILE)], fresh)

        tiles(forward)
        load.wni.wait()
        agg = s.agg[...].astype(bf16)
        s.agg_b[...] = agg
        npre = dot(own[...], w_n1[...]) + dot(agg, w_n2[...]) + given.nshift[...]
        nhid, ndact = silu_parts(npre)
        nhid = nhid.astype(bf16)
        s.nhid[...] = nhid
        load.wno.wait()
        nlinear = dot(nhid, s.wno_v[...]) + given.noff[...]
        nnormed, ninvstd = layer_norm(nlinear)
        load.ncot.wait()
        cotan = s.ncot_v[...].astype(f32)
        lback = norm_back(cotan, nnormed, ninvstd, given.ngain[...])
        lhalf = lback.astype(bf16)
        s.lhalf[...] = lhalf
        pback = dot_nt(lhalf, s.wno_v[...]) * ndact
        phalf = pback.astype(bf16)
        s.phalf[...] = phalf
        s.back_b[...] = dot_nt(phalf, w_n2[...]).astype(bf16)
        for row, values in ((3, pback), (4, lback), (5, cotan * nnormed)):
            total = jnp.sum(column_sums(values), axis=0, keepdims=True) * node_norm
            bufs.vc[0, pl.ds(row, 1)] = total
        bufs.vc[0, pl.ds(6, 2)] = jnp.zeros((2, WIDTH), f32)
        for j in range(2):
            cols = pl.ds(256 * j, 256)
            flat[pl.ds(2048 + 256 * j, 256)] = dot_tn(s.look[pl.ds(0, NODES), cols], phalf) * node_norm
            flat[pl.ds(2560 + 256 * j, 256)] = dot_tn(s.agg_b[:, cols], phalf) * node_norm
            flat[pl.ds(3072 + 256 * j, 256)] = dot_tn(s.nhid[:, cols], lhalf) * node_norm
        red.round_blocks(0)
        red.core_start(0)
        s.sums[...] = jnp.zeros((3, 8, WIDTH), f32)
        load.ecot.wait()

        def upstream(rows):
            return s.ecot_v[rows].astype(f32) + dot(s.pick[rows, pl.ds(0, NODES)], s.back_b[...])

        def backward_one(i):
            rows = pl.ds(i, TILE)
            fresh_back = upstream(rows)
            s.pre[rows] = fresh_back
            normed = s.normed[rows]
            eback = norm_back(fresh_back, normed, s.invstd[rows, pl.ds(0, 1)], given.egain[...])
            s.elhalf[rows] = eback.astype(bf16)
            s.sums[1] += column_sums(eback)
            s.sums[2] += column_sums(fresh_back * normed)

        tiles(backward_one)
        red.first_start(0)

        def grow(left, right, row, scale, count=2):
            def body(j):
                cols = pl.ds(pl.multiple_of(j, 256), 256)
                flat[pl.ds(pl.multiple_of(row + j, 64), 256)] = dot_tn(left[:, cols], right[...]) * scale

            chunks(256 * count, 256, body)

        grow(s.hidden, s.elhalf, 1536, edge_norm)
        red.round_blocks(1)
        red.core_start(1)

        def backward_two(i):
            rows = pl.ds(i, TILE)
            epback = dot_nt(s.elhalf[rows], s.weo_v[...]) * s.dact[rows]
            s.ephalf[rows] = epback.astype(bf16)
            s.sums[0] += column_sums(epback)

        tiles(backward_two)
        for row in range(3):
            bufs.vc[0, pl.ds(row, 1)] = jnp.sum(s.sums[row], axis=0, keepdims=True) * edge_norm
        red.vector_start(0)
        red.first_start(1)
        grow(s.edges_v, s.ephalf, 0, edge_norm)

        def gather(i):
            rows = pl.ds(i, 128)
            s.gathered[rows] = dot(s.pick_t[rows], s.ephalf[...]).astype(bf16)

        chunks(PICKS, 128, gather)
        r_rows, s_rows = pl.ds(0, NODES), pl.ds(NODES, LOOKUP)
        grow(s.look, s.gathered.at[s_rows], 512, edge_norm)
        grow(s.look.at[r_rows], s.gathered.at[r_rows], 1024, edge_norm)
        red.round_blocks(2)
        red.core_start(2)
        s.rim[...] = dot_nt(s.gathered[pl.ds(2 * NODES, 2 * SLOTS)], w_s[...]).astype(bf16)
        rims = [
            send(s.rim.at[pl.ds(0, SLOTS)], s.back.at[pl.ds(SLOTS, SLOTS)], s.hs.at[2], s.hq.at[2], beside(-1)),
            send(s.rim.at[pl.ds(SLOTS, SLOTS)], s.back.at[pl.ds(0, SLOTS)], s.hs.at[3], s.hq.at[3], beside(1)),
        ]
        for copy in rims:
            copy.start()
        red.vector_start(1, red.vector_value(0))
        red.second_y_start(0)

        def edge_grads(i):
            rows = pl.ds(i, TILE)
            ge_out[rows] = (s.pre[rows] + dot_nt(s.ephalf[rows], w_e[...])).astype(bf16)

        edge_grads(0)
        red.first_start(2)
        red.second_y_start(1)
        red.vector_start(2, red.vector_value(1))
        edge_grads(TILE)
        s.gnodes[...] = (
            s.ncot_v[...].astype(f32)
            + dot_nt(s.phalf[...], w_n1[...])
            + dot_nt(s.gathered[r_rows], w_r[...])
            + dot_nt(s.gathered[pl.ds(NODES, NODES)], w_s[...])
        )
        for copy in rims:
            copy.wait_recv()
        gn_out[...] = s.gnodes[...] + dot(send_t, s.back[...])
        red.second_y_start(2)
        red.second_x_start()
        red.vector_start(3, red.vector_value(2))
        red.third_start()
        sums = red.vector_value(3)
        for j in range(WIDTH // 128):
            v_out[pl.ds(j, 6, stride=WIDTH // 128), :] = sums[0:6, 128 * j : 128 * j + 128]
        red.finish(w_out)
        red.drain()
        red.vector_drain()
        for copy in halo + rims:
            copy.wait_send()

    hbm_spec = pl.BlockSpec(memory_space=pltpu.HBM)
    vmem_spec = pl.BlockSpec(memory_space=pltpu.VMEM)
    return pl.pallas_call(
        kernel,
        out_shape=(
            jax.ShapeDtypeStruct((NODES, WIDTH), jnp.float32),
            jax.ShapeDtypeStruct((EDGES, WIDTH), jnp.bfloat16),
            jax.ShapeDtypeStruct((SHARE * WIDTH // 128, 128), jnp.float32),
            jax.ShapeDtypeStruct((6 * WIDTH // 128, 128), jnp.float32),
        ),
        in_specs=[hbm_spec] * 17,
        out_specs=(vmem_spec, vmem_spec, vmem_spec, vmem_spec),
        scratch_shapes=[*compute_scratch().values(), *reduce_scratch().values()],
        compiler_params=pltpu.CompilerParams(
            collective_id=0, has_side_effects=True, vmem_limit_bytes=60 * 1024 * 1024
        ),
        name="layer_back",
    )(*operands)


def store(*values):
    count = len(values)

    def kernel(*refs):
        sems = refs[2 * count]
        copies = [pltpu.make_async_copy(refs[i], refs[count + i], sems.at[i]) for i in range(count)]
        for copy in copies:
            copy.start()
        for copy in copies:
            copy.wait()

    return pl.pallas_call(
        kernel,
        out_shape=tuple(jax.ShapeDtypeStruct(value.shape, value.dtype) for value in values),
        in_specs=[pl.BlockSpec(memory_space=pltpu.VMEM)] * count,
        out_specs=(pl.BlockSpec(memory_space=pltpu.HBM),) * count,
        scratch_shapes=[pltpu.SemaphoreType.DMA((count,))],
        name="store",
    )(*values)


def per_device(
    nodes,
    edges,
    node_cotan,
    edge_cotan,
    edge_inner,
    edge_outer,
    node_inner,
    node_outer,
    edge_shift,
    edge_offset,
    edge_gain,
    node_shift,
    node_offset,
    node_gain,
    send_rows,
    senders,
    receivers,
):
    devices_all = lax.axis_size("region") * lax.axis_size("patch")
    edge_norm = 1.0 / math.sqrt(EDGES * devices_all)
    node_norm = 1.0 / math.sqrt(NODES * devices_all)
    vectors = (edge_shift, edge_offset, edge_gain, node_shift, node_offset, node_gain)
    grad_nodes, grad_edges, weights, vector_sums = layer(
        edge_norm,
        node_norm,
        nodes,
        edges,
        node_cotan,
        edge_cotan,
        edge_inner,
        edge_outer,
        node_inner,
        node_outer,
        *(vector.reshape(1, WIDTH) for vector in vectors),
        send_rows.reshape(2, SLOTS),
        senders.reshape(EDGES // 128, 128),
        receivers.reshape(EDGES // 128, 128),
    )
    grad_nodes, grad_edges, weights, vector_sums = store(grad_nodes, grad_edges, weights, vector_sums)
    return (grad_nodes, grad_edges, weights.reshape(-1), vector_sums.reshape(-1))


def solution(mesh):
    in_specs = (
        P(("region", "patch"), None),
        P(("region", "patch"), None),
        P(("region", "patch"), None),
        P(("region", "patch"), None),
        P(),
        P(),
        P(),
        P(),
        P(),
        P(),
        P(),
        P(),
        P(),
        P(),
        P("region", "patch", None, None),
        P(("region", "patch")),
        P(("region", "patch")),
    )
    out_specs = (
        P(("region", "patch"), None),
        P(("region", "patch"), None),
        P(("region", "patch")),
        P(),
    )
    return jax.shard_map(
        per_device, mesh=mesh, in_specs=in_specs, out_specs=out_specs, check_vma=False
    )
```

```python
import math
from types import SimpleNamespace

import jax
import jax.numpy as jnp
from jax import lax
from jax.experimental import pallas as pl
from jax.experimental.pallas import tpu as pltpu
from jax.sharding import PartitionSpec as P

MESH = pl.DeviceIdType.MESH
NX, NC, NY, NZ = 4, 2, 4, 8
WIDTH, XW, YW = 512, 128, 384
BLOCK, QUARTER, SHARE, PAD = 448, 112, 14, 16


def coordinates():
    region, patch = lax.axis_index("region"), lax.axis_index("patch")
    return region // NC, lax.rem(region, NC), patch // NZ, lax.rem(patch, NZ)


def at(x, c, y, z):
    return (x * NC + c, y * NZ + z)


def beside(step):
    region, patch = lax.axis_index("region"), lax.axis_index("patch")
    return (region, lax.rem(patch + step + NY * NZ, NY * NZ))


def peers():
    x, c, y, z = coordinates()
    found = [at(x, 1 - c, y, z), beside(1), beside(-1)]
    found += [at(lax.rem(x + k, NX), c, y, z) for k in range(1, NX)]
    found += [at(x, c, lax.rem(y + k, NY), z) for k in range(1, NY)]
    found += [at(x, c, y, lax.rem(z + k, NZ)) for k in range(1, NZ)]
    return found


def barrier_signal():
    barrier = pltpu.get_barrier_semaphore()
    for device in peers():
        pl.semaphore_signal(barrier, inc=1, device_id=device, device_id_type=MESH)


def barrier_wait():
    pl.semaphore_wait(pltpu.get_barrier_semaphore(), len(peers()))


def send(src, dst, send_sem, recv_sem, device):
    return pltpu.make_async_remote_copy(
        src_ref=src,
        dst_ref=dst,
        send_sem=send_sem,
        recv_sem=recv_sem,
        device_id=device,
        device_id_type=MESH,
    )


def waiter(ref, sem):
    x, c, y, z = coordinates()
    return send(ref, ref, sem, sem, at(x, 1 - c, y, z))


def chunks(total, step, body):
    def one(i, carry):
        body(pl.multiple_of(i * step, step))
        return carry

    lax.fori_loop(0, total // step, one, 0)


def reduce_scratch():
    bf16, f32 = jnp.bfloat16, jnp.float32
    dma = pltpu.SemaphoreType.DMA
    return dict(
        sb=pltpu.VMEM((NX, NC, BLOCK, WIDTH), bf16),
        r0=pltpu.VMEM((NX, BLOCK, WIDTH), bf16),
        b1=pltpu.VMEM((NX, BLOCK, WIDTH), bf16),
        r1x=pltpu.VMEM((NX, BLOCK, XW), bf16),
        r1y=pltpu.VMEM((NY, NX, QUARTER, YW), bf16),
        a1x=pltpu.VMEM((NY, QUARTER, XW), f32),
        b2x=pltpu.VMEM((NY, QUARTER, XW), bf16),
        r2x=pltpu.VMEM((NY, QUARTER, XW), bf16),
        a1y=pltpu.VMEM((NX, QUARTER, YW), f32),
        b2y=pltpu.VMEM((NX, QUARTER, YW), bf16),
        r2y=pltpu.VMEM((NX, QUARTER, YW), bf16),
        packed=pltpu.VMEM((NZ, PAD, XW + YW), f32),
        b3=pltpu.VMEM((NZ, PAD, XW + YW), bf16),
        r3=pltpu.VMEM((NZ, PAD, XW + YW), bf16),
        sent=dma((6,)),
        q0=dma((NX,)),
        q1x=dma,
        q1y=dma((NX,)),
        q2x=dma,
        q2y=dma,
        q3=dma,
        vc=pltpu.VMEM((2, 8, WIDTH), f32),
        vx=pltpu.VMEM((NX, 8, WIDTH), f32),
        vy=pltpu.VMEM((NY, 8, WIDTH), f32),
        vz=pltpu.VMEM((NZ, 8, WIDTH), f32),
        us=dma((4,)),
        uq=dma((4,)),
    )


class Reducer:
    def __init__(self, g, bufs):
        self.g, self.b = g, bufs
        self.x, self.c, self.y, self.z = coordinates()
        self.piece_xs = ((3,), (2,), (0,), (1,))

    def core_copies(self, piece):
        b = self.b
        return [
            send(
                b.sb.at[xx, 1 - self.c],
                b.r0.at[xx],
                b.sent.at[0],
                b.q0.at[xx],
                at(self.x, 1 - self.c, self.y, self.z),
            )
            for xx in self.piece_xs[piece]
        ]

    def core_start(self, piece):
        for copy in self.core_copies(piece):
            copy.start()

    def round_blocks(self, piece):
        b, g = self.b, self.g
        for xx in self.piece_xs[piece]:

            def body(i, xx=xx):
                b.sb[xx, 1 - self.c, pl.ds(i, 64)] = g[xx, 1 - self.c, pl.ds(i, 64)].astype(jnp.bfloat16)

            chunks(BLOCK, 64, body)

    def first_x(self, xx):
        b = self.b
        return send(
            b.b1.at[xx, :, pl.ds(0, XW)],
            b.r1x.at[self.x],
            b.sent.at[1],
            b.q1x,
            at(xx, self.c, self.y, self.z),
        )

    def first_y(self, piece, k):
        b = self.b
        to = lax.rem(self.y + k, NY)
        xs = self.piece_xs[piece]
        blocks = pl.ds(xs[0], len(xs))
        return send(
            b.b1.at[blocks, pl.ds(pl.multiple_of(to * QUARTER, 16), QUARTER), pl.ds(XW, YW)],
            b.r1y.at[k, blocks],
            b.sent.at[2],
            b.q1y.at[xs[0]],
            at(self.x, self.c, to, self.z),
        )

    def first_start(self, piece):
        b, g = self.b, self.g
        for copy in self.core_copies(piece):
            copy.wait_recv()
        for xx in self.piece_xs[piece]:

            def body(i, xx=xx):
                total = g[xx, self.c, pl.ds(i, 64)] + b.r0[xx, pl.ds(i, 64)].astype(jnp.float32)
                g[xx, self.c, pl.ds(i, 64)] = total
                b.b1[xx, pl.ds(i, 64)] = total.astype(jnp.bfloat16)

            chunks(BLOCK, 64, body)
        for k in (2, 1, 3):
            self.first_y(piece, k).start()
        for xx in self.piece_xs[piece]:

            @pl.when(self.x != xx)
            def _(xx=xx):
                self.first_x(xx).start()

    def second_x(self, k):
        b = self.b
        to = lax.rem(self.y + k, NY)
        return send(
            b.b2x.at[to],
            b.r2x.at[k],
            b.sent.at[3],
            b.q2x,
            at(self.x, self.c, to, self.z),
        )

    def second_y(self, xx):
        b = self.b
        return send(
            b.b2y.at[xx],
            b.r2y.at[self.x],
            b.sent.at[4],
            b.q2y,
            at(xx, self.c, self.y, self.z),
        )

    def second_y_start(self, piece):
        b, g = self.b, self.g
        for xx in self.piece_xs[piece]:
            waiter(b.r1y.at[pl.ds(1, NY - 1), xx], b.q1y.at[xx]).wait_recv()
        base = self.y * QUARTER
        for xx in self.piece_xs[piece]:

            def body(i, xx=xx):
                total = g[xx, self.c, pl.ds(pl.multiple_of(base + i, 16), 16), pl.ds(XW, YW)]
                for k in range(1, NY):
                    total += b.r1y[k, xx, pl.ds(i, 16)].astype(jnp.float32)
                b.a1y[xx, pl.ds(i, 16)] = total
                b.b2y[xx, pl.ds(i, 16)] = total.astype(jnp.bfloat16)

            chunks(QUARTER, 16, body)
        for xx in self.piece_xs[piece]:

            @pl.when(self.x != xx)
            def _(xx=xx):
                self.second_y(xx).start()

    def second_x_start(self):
        b, g = self.b, self.g
        waiter(b.r1x.at[pl.ds(0, NX - 1)], b.q1x).wait_recv()
        for yy in range(NY):

            def body(i, yy=yy):
                total = g[self.x, self.c, pl.ds(yy * QUARTER + i, 16), pl.ds(0, XW)]
                for k in range(1, NX):
                    source = lax.rem(self.x + k, NX)
                    total += b.r1x[source, pl.ds(yy * QUARTER + i, 16)].astype(jnp.float32)
                b.a1x[yy, pl.ds(i, 16)] = total
                b.b2x[yy, pl.ds(i, 16)] = total.astype(jnp.bfloat16)

            chunks(QUARTER, 16, body)
        for k in (2, 1, 3):
            self.second_x(k).start()

    def third(self, k):
        b = self.b
        to = lax.rem(self.z + k, NZ)
        return send(
            b.b3.at[to],
            b.r3.at[k],
            b.sent.at[5],
            b.q3,
            at(self.x, self.c, self.y, to),
        )

    def third_start(self):
        b = self.b
        waiter(b.r2x.at[pl.ds(1, NY - 1)], b.q2x).wait_recv()
        waiter(b.r2y.at[pl.ds(0, NX - 1)], b.q2y).wait_recv()
        for i in range(NZ):
            rows = pl.ds(i * SHARE, SHARE)
            left = b.a1x[self.y, rows]
            right = b.a1y[self.x, rows]
            for k in range(1, NY):
                left += b.r2x[k, rows].astype(jnp.float32)
                right += b.r2y[lax.rem(self.x + k, NX), rows].astype(jnp.float32)
            both = jnp.concatenate([left, right], axis=1)
            b.packed[i, pl.ds(0, SHARE)] = both
            b.b3[i, pl.ds(0, SHARE)] = both.astype(jnp.bfloat16)
        for k in (4, 3, 5, 2, 6, 1, 7):
            self.third(k).start()

    def finish(self, out):
        b = self.b
        waiter(b.r3.at[pl.ds(1, NZ - 1)], b.q3).wait_recv()
        total = b.packed[self.z, pl.ds(0, SHARE)]
        for k in range(1, NZ):
            total += b.r3[k, pl.ds(0, SHARE)].astype(jnp.float32)
        for j in range(WIDTH // 128):
            out[pl.ds(j, SHARE, stride=4), :] = total[:, 128 * j : 128 * j + 128]

    def drain(self):
        b = self.b
        for i, ref in enumerate(
            (
                b.r0,
                b.r1x.at[pl.ds(0, NX - 1)],
                b.r1y.at[pl.ds(1, NY - 1)],
                b.r2x.at[pl.ds(1, NY - 1)],
                b.r2y.at[pl.ds(0, NX - 1)],
                b.r3.at[pl.ds(1, NZ - 1)],
            )
        ):
            waiter(ref, b.sent.at[i]).wait_send()

    def vector_copies(self, stage):
        b = self.b
        x, c, y, z = self.x, self.c, self.y, self.z
        if stage == 0:
            return [send(b.vc.at[0], b.vc.at[1], b.us.at[0], b.uq.at[0], at(x, 1 - c, y, z))]
        buf, count, me = ((b.vx, NX, x), (b.vy, NY, y), (b.vz, NZ, z))[stage - 1]
        found = []
        for k in range(1, count):
            to = lax.rem(me + k, count)
            device = (at(to, c, y, z), at(x, c, to, z), at(x, c, y, to))[stage - 1]
            found.append(send(buf.at[me], buf.at[me], b.us.at[stage], b.uq.at[stage], device))
        return found

    def vector_bytes(self, stage):
        b = self.b
        if stage == 0:
            return b.vc.at[1]
        buf, count = ((b.vx, NX), (b.vy, NY), (b.vz, NZ))[stage - 1]
        return buf.at[pl.ds(0, count - 1)]

    def vector_start(self, stage, value=None):
        b = self.b
        if stage > 0:
            (b.vx, b.vy, b.vz)[stage - 1][(self.x, self.y, self.z)[stage - 1]] = value
        for copy in self.vector_copies(stage):
            copy.start()

    def vector_value(self, stage):
        b = self.b
        waiter(self.vector_bytes(stage), b.uq.at[stage]).wait_recv()
        if stage == 0:
            return b.vc[0] + b.vc[1]
        buf = (b.vx, b.vy, b.vz)[stage - 1]
        total = buf[0]
        for i in range(1, buf.shape[0]):
            total += buf[i]
        return total

    def vector_drain(self):
        for stage in range(4):
            waiter(self.vector_bytes(stage), self.b.us.at[stage]).wait_send()


NODES, EDGES, SLOTS, LOOKUP, PICKS = 256, 1024, 32, 320, 640
TILE = 512


def dot(left, right):
    return jnp.dot(left, right, preferred_element_type=jnp.float32)


def dot_nt(left, right):
    return lax.dot_general(left, right, (((1,), (1,)), ((), ())), preferred_element_type=jnp.float32)


def dot_tn(left, right):
    return lax.dot_general(left, right, (((0,), (0,)), ((), ())), preferred_element_type=jnp.float32)


def layer_norm(values):
    centred = values - jnp.mean(values, axis=-1, keepdims=True)
    invstd = lax.rsqrt(jnp.mean(centred * centred, axis=-1, keepdims=True) + 1e-05)
    return centred * invstd, invstd


def norm_back(upstream, normed, invstd, gains):
    scaled = upstream * gains
    return invstd * (
        scaled
        - jnp.mean(scaled, axis=-1, keepdims=True)
        - normed * jnp.mean(scaled * normed, axis=-1, keepdims=True)
    )


def silu_parts(preact):
    sigmoid = 1.0 / (1.0 + jnp.exp(-preact))
    hidden = preact * sigmoid
    return hidden, sigmoid + hidden * (1.0 - sigmoid)


def column_sums(values):
    return jnp.sum(values.reshape(-1, 8, WIDTH), axis=0)


def operands_named(
    nodes, edges, ncot, ecot, wei, weo, wni, wno, eshift, eoff, egain, nshift, noff, ngain, sendid, sndid, rcvid
):
    return SimpleNamespace(**locals())


SMALL = ("eshift", "eoff", "egain", "nshift", "noff", "ngain", "sendid", "sndid", "rcvid")


def compute_scratch():
    bf16, f32 = jnp.bfloat16, jnp.float32
    vm, dma = pltpu.VMEM, pltpu.SemaphoreType.DMA
    return dict(
        g=vm((NX, NC, BLOCK, WIDTH), f32),
        look=vm((LOOKUP, WIDTH), bf16),
        edges_v=vm((EDGES, WIDTH), bf16),
        ncot_v=vm((NODES, WIDTH), bf16),
        ecot_v=vm((EDGES, WIDTH), bf16),
        wei_v=vm((3 * WIDTH, WIDTH), bf16),
        weo_v=vm((WIDTH, WIDTH), bf16),
        wni_v=vm((2 * WIDTH, WIDTH), bf16),
        wno_v=vm((WIDTH, WIDTH), bf16),
        eshift_v=vm((1, WIDTH), f32),
        eoff_v=vm((1, WIDTH), f32),
        egain_v=vm((1, WIDTH), f32),
        nshift_v=vm((1, WIDTH), f32),
        noff_v=vm((1, WIDTH), f32),
        ngain_v=vm((1, WIDTH), f32),
        sendid_v=vm((2, SLOTS), jnp.int32),
        sndid_v=vm((EDGES // 128, 128), jnp.int32),
        rcvid_v=vm((EDGES // 128, 128), jnp.int32),
        loads=dma((18,)),
        pick=vm((EDGES, PICKS), bf16),
        pick_t=vm((PICKS, EDGES), bf16),
        proj=vm((PICKS, WIDTH), bf16),
        outgoing=vm((2 * SLOTS, WIDTH), bf16),
        pre=vm((EDGES, WIDTH), f32),
        dact=vm((EDGES, WIDTH), f32),
        hidden=vm((EDGES, WIDTH), bf16),
        normed=vm((EDGES, WIDTH), f32),
        invstd=vm((EDGES, 128), f32),
        agg=vm((NODES, WIDTH), f32),
        agg_b=vm((NODES, WIDTH), bf16),
        back_b=vm((NODES, WIDTH), bf16),
        nhid=vm((NODES, WIDTH), bf16),
        lhalf=vm((NODES, WIDTH), bf16),
        phalf=vm((NODES, WIDTH), bf16),
        elhalf=vm((EDGES, WIDTH), bf16),
        ephalf=vm((EDGES, WIDTH), bf16),
        gathered=vm((PICKS, WIDTH), bf16),
        rim=vm((2 * SLOTS, WIDTH), bf16),
        back=vm((2 * SLOTS, WIDTH), bf16),
        gnodes=vm((NODES, WIDTH), f32),
        sums=vm((3, 8, WIDTH), f32),
        hs=dma((4,)),
        hq=dma((4,)),
    )


def layer(edge_norm, node_norm, *operands):
    names = list(compute_scratch())
    comm_names = list(reduce_scratch())

    def kernel(*refs):
        given = operands_named(*refs[:17])
        gn_out, ge_out, w_out, v_out = refs[17:21]
        s = SimpleNamespace(**dict(zip(names, refs[21 : 21 + len(names)])))
        bufs = SimpleNamespace(**dict(zip(comm_names, refs[21 + len(names) :])))
        bf16, f32 = jnp.bfloat16, jnp.float32
        barrier_signal()
        red = Reducer(s.g, bufs)
        flat = s.g.reshape(NX * NC * BLOCK, WIDTH)
        wei = given.wei
        loads = dict(
            ecot=(given.ecot, s.ecot_v),
            ncot=(given.ncot, s.ncot_v),
            wno=(given.wno, s.wno_v),
            wni=(given.wni, s.wni_v),
            weo=(given.weo, s.weo_v),
            ws=(wei.at[pl.ds(WIDTH, 2 * WIDTH)], s.wei_v.at[pl.ds(WIDTH, 2 * WIDTH)]),
            edges=(given.edges, s.edges_v),
            we=(wei.at[pl.ds(0, WIDTH)], s.wei_v.at[pl.ds(0, WIDTH)]),
            nodes=(given.nodes, s.look.at[pl.ds(0, NODES)]),
        )
        for name in SMALL:
            loads[name] = (getattr(given, name), getattr(s, name + "_v"))
            setattr(given, name, getattr(s, name + "_v"))
        load = {}
        for i, (name, (src, dst)) in enumerate(reversed(loads.items())):
            load[name] = pltpu.make_async_copy(src, dst, s.loads.at[i])
            load[name].start()
        load = SimpleNamespace(**load)
        w_e = s.wei_v.at[pl.ds(0, WIDTH)]
        w_s = s.wei_v.at[pl.ds(WIDTH, WIDTH)]
        w_r = s.wei_v.at[pl.ds(2 * WIDTH, WIDTH)]
        w_n1 = s.wni_v.at[pl.ds(0, WIDTH)]
        w_n2 = s.wni_v.at[pl.ds(WIDTH, WIDTH)]
        own = s.look.at[pl.ds(0, NODES)]

        for name in SMALL:
            getattr(load, name).wait()

        def one(mask):
            return jnp.where(mask, 1.0, 0.0).astype(bf16)

        send_ids = jnp.concatenate([given.sendid[0:1, :], given.sendid[1:2, :]], axis=1)
        send_t = one(lax.broadcasted_iota(jnp.int32, (NODES, 2 * SLOTS), 0) == send_ids)
        s.proj[pl.ds(NODES + LOOKUP, 64)] = jnp.zeros((64, WIDTH), bf16)

        load.nodes.wait()
        s.outgoing[...] = dot_tn(send_t, own[...]).astype(bf16)
        halo = [
            send(s.outgoing.at[pl.ds(0, SLOTS)], s.look.at[pl.ds(NODES + SLOTS, SLOTS)], s.hs.at[0], s.hq.at[0], beside(-1)),
            send(s.outgoing.at[pl.ds(SLOTS, SLOTS)], s.look.at[pl.ds(NODES, SLOTS)], s.hs.at[1], s.hq.at[1], beside(1)),
        ]
        barrier_wait()
        for copy in halo:
            copy.start()

        for j in range(EDGES // 128):
            lanes = pl.ds(128 * j, 128)
            snd, rcv = given.sndid[j : j + 1, :], given.rcvid[j : j + 1, :]
            s.pick_t[pl.ds(0, NODES), lanes] = one(lax.broadcasted_iota(jnp.int32, (NODES, 128), 0) == rcv)
            s.pick_t[pl.ds(NODES, PICKS - NODES), lanes] = one(
                lax.broadcasted_iota(jnp.int32, (PICKS - NODES, 128), 0) == snd
            )
            snd_c = jnp.broadcast_to(snd, (128, 128)).T
            rcv_c = jnp.broadcast_to(rcv, (128, 128)).T
            lane = lax.broadcasted_iota(jnp.int32, (128, 128), 1)
            for i in range(2):
                s.pick[pl.ds(128 * j, 128), pl.ds(128 * i, 128)] = one(rcv_c == lane + 128 * i)
            for i in range(3):
                s.pick[pl.ds(128 * j, 128), pl.ds(NODES + 128 * i, 128)] = one(snd_c == lane + 128 * i)
        def tiles(body):
            chunks(EDGES, TILE, body)

        load.we.wait()
        load.edges.wait()

        def first(i):
            rows = pl.ds(i, TILE)
            s.pre[rows] = dot(s.edges_v[rows], w_e[...]) + given.eshift[...]

        tiles(first)
        load.ws.wait()
        s.proj[pl.ds(0, NODES)] = dot(own[...], w_r[...]).astype(bf16)
        for copy in halo:
            copy.wait_recv()
        s.proj[pl.ds(NODES, LOOKUP)] = dot(s.look[...], w_s[...]).astype(bf16)
        load.weo.wait()
        s.agg[...] = jnp.zeros((NODES, WIDTH), f32)

        def forward(i):
            rows = pl.ds(i, TILE)
            preact = s.pre[rows] + dot(s.pick[rows], s.proj[...])
            hidden, dact = silu_parts(preact)
            s.dact[rows] = dact
            hidden = hidden.astype(bf16)
            s.hidden[rows] = hidden
            linear = dot(hidden, s.weo_v[...]) + given.eoff[...]
            normed, invstd = layer_norm(linear)
            s.normed[rows] = normed
            s.invstd[rows] = jnp.broadcast_to(invstd, (TILE, 128))
            fresh = (s.edges_v[rows].astype(f32) + given.egain[...] * normed).astype(bf16)
            s.agg[...] += dot(s.pick_t[pl.ds(0, NODES), pl.ds(i, TILE)], fresh)

        tiles(forward)
        load.wni.wait()
        agg = s.agg[...].astype(bf16)
        s.agg_b[...] = agg
        npre = dot(own[...], w_n1[...]) + dot(agg, w_n2[...]) + given.nshift[...]
        nhid, ndact = silu_parts(npre)
        nhid = nhid.astype(bf16)
        s.nhid[...] = nhid
        load.wno.wait()
        nlinear = dot(nhid, s.wno_v[...]) + given.noff[...]
        nnormed, ninvstd = layer_norm(nlinear)
        load.ncot.wait()
        cotan = s.ncot_v[...].astype(f32)
        lback = norm_back(cotan, nnormed, ninvstd, given.ngain[...])
        lhalf = lback.astype(bf16)
        s.lhalf[...] = lhalf
        pback = dot_nt(lhalf, s.wno_v[...]) * ndact
        phalf = pback.astype(bf16)
        s.phalf[...] = phalf
        s.back_b[...] = dot_nt(phalf, w_n2[...]).astype(bf16)
        for row, values in ((3, pback), (4, lback), (5, cotan * nnormed)):
            total = jnp.sum(column_sums(values), axis=0, keepdims=True) * node_norm
            bufs.vc[0, pl.ds(row, 1)] = total
        bufs.vc[0, pl.ds(6, 2)] = jnp.zeros((2, WIDTH), f32)
        s.sums[...] = jnp.zeros((3, 8, WIDTH), f32)
        load.ecot.wait()

        def upstream(rows):
            return s.ecot_v[rows].astype(f32) + dot(s.pick[rows, pl.ds(0, NODES)], s.back_b[...])

        def backward_one(i):
            rows = pl.ds(i, TILE)
            fresh_back = upstream(rows)
            s.pre[rows] = fresh_back
            normed = s.normed[rows]
            eback = norm_back(fresh_back, normed, s.invstd[rows, pl.ds(0, 1)], given.egain[...])
            s.elhalf[rows] = eback.astype(bf16)
            s.sums[1] += column_sums(eback)
            s.sums[2] += column_sums(fresh_back * normed)
            j = i // TILE * 256
            cols = pl.ds(j if isinstance(j, int) else pl.multiple_of(j, 256), 256)
            flat[pl.ds(2048 + j, 256)] = dot_tn(s.look[pl.ds(0, NODES), cols], s.phalf[...]) * node_norm
            flat[pl.ds(2560 + j, 256)] = dot_tn(s.agg_b[:, cols], s.phalf[...]) * node_norm
            flat[pl.ds(3072 + j, 256)] = dot_tn(s.nhid[:, cols], s.lhalf[...]) * node_norm

        tiles(backward_one)
        red.round_blocks(0)
        red.core_start(0)

        def grow(left, right, row, scale, count=2):
            def body(j):
                cols = pl.ds(pl.multiple_of(j, 256), 256)
                flat[pl.ds(pl.multiple_of(row + j, 64), 256)] = dot_tn(left[:, cols], right[...]) * scale

            chunks(256 * count, 256, body)

        grow(s.hidden, s.elhalf, 1536, edge_norm)
        red.first_start(0)
        red.round_blocks(1)
        red.core_start(1)

        def backward_two(i):
            rows = pl.ds(i, TILE)
            epback = dot_nt(s.elhalf[rows], s.weo_v[...]) * s.dact[rows]
            s.ephalf[rows] = epback.astype(bf16)
            s.sums[0] += column_sums(epback)

        tiles(backward_two)
        for row in range(3):
            bufs.vc[0, pl.ds(row, 1)] = jnp.sum(s.sums[row], axis=0, keepdims=True) * edge_norm
        red.vector_start(0)
        red.first_start(1)
        grow(s.edges_v, s.ephalf, 0, edge_norm)

        live = pl.ds(0, NODES + LOOKUP)
        s.gathered[live] = dot(s.pick_t[live], s.ephalf[...]).astype(bf16)
        r_rows, s_rows = pl.ds(0, NODES), pl.ds(NODES, LOOKUP)
        grow(s.look, s.gathered.at[s_rows], 512, edge_norm)
        red.round_blocks(2)
        red.core_start(2)
        grow(s.look.at[r_rows], s.gathered.at[r_rows], 1024, edge_norm)
        red.round_blocks(3)
        red.core_start(3)
        s.rim[...] = dot_nt(s.gathered[pl.ds(2 * NODES, 2 * SLOTS)], w_s[...]).astype(bf16)
        rims = [
            send(s.rim.at[pl.ds(0, SLOTS)], s.back.at[pl.ds(SLOTS, SLOTS)], s.hs.at[2], s.hq.at[2], beside(-1)),
            send(s.rim.at[pl.ds(SLOTS, SLOTS)], s.back.at[pl.ds(0, SLOTS)], s.hs.at[3], s.hq.at[3], beside(1)),
        ]
        for copy in rims:
            copy.start()
        red.vector_start(1, red.vector_value(0))

        def edge_grads(i):
            rows = pl.ds(i, TILE)
            ge_out[rows] = (s.pre[rows] + dot_nt(s.ephalf[rows], w_e[...])).astype(bf16)

        red.first_start(2)
        red.first_start(3)
        red.vector_start(2, red.vector_value(1))
        for piece in range(2):
            red.second_y_start(piece)
        edge_grads(0)
        edge_grads(TILE)
        s.gnodes[...] = (
            s.ncot_v[...].astype(f32)
            + dot_nt(s.phalf[...], w_n1[...])
            + dot_nt(s.gathered[r_rows], w_r[...])
            + dot_nt(s.gathered[pl.ds(NODES, NODES)], w_s[...])
        )
        for copy in rims:
            copy.wait_recv()
        gn_out[...] = s.gnodes[...] + dot(send_t, s.back[...])
        red.second_y_start(2)
        red.second_y_start(3)
        red.second_x_start()
        red.vector_start(3, red.vector_value(2))
        red.third_start()
        sums = red.vector_value(3)
        for j in range(WIDTH // 128):
            v_out[pl.ds(j, 6, stride=WIDTH // 128), :] = sums[0:6, 128 * j : 128 * j + 128]
        red.finish(w_out)
        red.drain()
        red.vector_drain()
        for copy in halo + rims:
            copy.wait_send()

    hbm_spec = pl.BlockSpec(memory_space=pltpu.HBM)
    vmem_spec = pl.BlockSpec(memory_space=pltpu.VMEM)
    return pl.pallas_call(
        kernel,
        out_shape=(
            jax.ShapeDtypeStruct((NODES, WIDTH), jnp.float32),
            jax.ShapeDtypeStruct((EDGES, WIDTH), jnp.bfloat16),
            jax.ShapeDtypeStruct((SHARE * WIDTH // 128, 128), jnp.float32),
            jax.ShapeDtypeStruct((6 * WIDTH // 128, 128), jnp.float32),
        ),
        in_specs=[hbm_spec] * 17,
        out_specs=(vmem_spec, vmem_spec, vmem_spec, vmem_spec),
        scratch_shapes=[*compute_scratch().values(), *reduce_scratch().values()],
        compiler_params=pltpu.CompilerParams(
            collective_id=0, has_side_effects=True, vmem_limit_bytes=60 * 1024 * 1024
        ),
        name="layer_back",
    )(*operands)


def store(*values):
    count = len(values)

    def kernel(*refs):
        sems = refs[2 * count]
        copies = [pltpu.make_async_copy(refs[i], refs[count + i], sems.at[i]) for i in range(count)]
        for copy in copies:
            copy.start()
        for copy in copies:
            copy.wait()

    return pl.pallas_call(
        kernel,
        out_shape=tuple(jax.ShapeDtypeStruct(value.shape, value.dtype) for value in values),
        in_specs=[pl.BlockSpec(memory_space=pltpu.VMEM)] * count,
        out_specs=(pl.BlockSpec(memory_space=pltpu.HBM),) * count,
        scratch_shapes=[pltpu.SemaphoreType.DMA((count,))],
        name="store",
    )(*values)


def per_device(
    nodes,
    edges,
    node_cotan,
    edge_cotan,
    edge_inner,
    edge_outer,
    node_inner,
    node_outer,
    edge_shift,
    edge_offset,
    edge_gain,
    node_shift,
    node_offset,
    node_gain,
    send_rows,
    senders,
    receivers,
):
    devices_all = lax.axis_size("region") * lax.axis_size("patch")
    edge_norm = 1.0 / math.sqrt(EDGES * devices_all)
    node_norm = 1.0 / math.sqrt(NODES * devices_all)
    vectors = (edge_shift, edge_offset, edge_gain, node_shift, node_offset, node_gain)
    grad_nodes, grad_edges, weights, vector_sums = layer(
        edge_norm,
        node_norm,
        nodes,
        edges,
        node_cotan,
        edge_cotan,
        edge_inner,
        edge_outer,
        node_inner,
        node_outer,
        *(vector.reshape(1, WIDTH) for vector in vectors),
        send_rows.reshape(2, SLOTS),
        senders.reshape(EDGES // 128, 128),
        receivers.reshape(EDGES // 128, 128),
    )
    grad_nodes, grad_edges, weights, vector_sums = store(grad_nodes, grad_edges, weights, vector_sums)
    return (grad_nodes, grad_edges, weights.reshape(-1), vector_sums.reshape(-1))


def solution(mesh):
    in_specs = (
        P(("region", "patch"), None),
        P(("region", "patch"), None),
        P(("region", "patch"), None),
        P(("region", "patch"), None),
        P(),
        P(),
        P(),
        P(),
        P(),
        P(),
        P(),
        P(),
        P(),
        P(),
        P("region", "patch", None, None),
        P(("region", "patch")),
        P(("region", "patch")),
    )
    out_specs = (
        P(("region", "patch"), None),
        P(("region", "patch"), None),
        P(("region", "patch")),
        P(),
    )
    return jax.shard_map(
        per_device, mesh=mesh, in_specs=in_specs, out_specs=out_specs, check_vma=False
    )
```

```python
import math
from types import SimpleNamespace

import jax
import jax.numpy as jnp
from jax import lax
from jax.experimental import pallas as pl
from jax.experimental.pallas import tpu as pltpu
from jax.sharding import PartitionSpec as P

MESH = pl.DeviceIdType.MESH
NX, NC, NY, NZ = 4, 2, 4, 8
WIDTH, XW, YW, ZW = 512, 128, 256, 128
BLOCK, QUARTER, SHARE, PAD = 448, 112, 14, 16


def coordinates():
    region, patch = lax.axis_index("region"), lax.axis_index("patch")
    return region // NC, lax.rem(region, NC), patch // NZ, lax.rem(patch, NZ)


def at(x, c, y, z):
    return (x * NC + c, y * NZ + z)


def beside(step):
    region, patch = lax.axis_index("region"), lax.axis_index("patch")
    return (region, lax.rem(patch + step + NY * NZ, NY * NZ))


def peers():
    x, c, y, z = coordinates()
    found = [at(x, 1 - c, y, z), beside(1), beside(-1)]
    found += [at(lax.rem(x + k, NX), c, y, z) for k in range(1, NX)]
    found += [at(x, c, lax.rem(y + k, NY), z) for k in range(1, NY)]
    found += [at(x, c, y, lax.rem(z + k, NZ)) for k in range(1, NZ)]
    return found


def barrier_signal():
    barrier = pltpu.get_barrier_semaphore()
    for device in peers():
        pl.semaphore_signal(barrier, inc=1, device_id=device, device_id_type=MESH)


def barrier_wait():
    pl.semaphore_wait(pltpu.get_barrier_semaphore(), len(peers()))


def send(src, dst, send_sem, recv_sem, device):
    return pltpu.make_async_remote_copy(
        src_ref=src,
        dst_ref=dst,
        send_sem=send_sem,
        recv_sem=recv_sem,
        device_id=device,
        device_id_type=MESH,
    )


def waiter(ref, sem):
    x, c, y, z = coordinates()
    return send(ref, ref, sem, sem, at(x, 1 - c, y, z))


def chunks(total, step, body):
    def one(i, carry):
        body(pl.multiple_of(i * step, step))
        return carry

    lax.fori_loop(0, total // step, one, 0)


def reduce_scratch():
    bf16, f32 = jnp.bfloat16, jnp.float32
    dma = pltpu.SemaphoreType.DMA
    return dict(
        sb=pltpu.VMEM((NX, NC, BLOCK, WIDTH), bf16),
        r0=pltpu.VMEM((NX, BLOCK, WIDTH), bf16),
        b1=pltpu.VMEM((NX, BLOCK, WIDTH), bf16),
        r1x=pltpu.VMEM((NX, BLOCK, XW), bf16),
        r1y=pltpu.VMEM((NY, NX, QUARTER, YW), bf16),
        a1x=pltpu.VMEM((NY, QUARTER, XW), f32),
        b2x=pltpu.VMEM((NY, QUARTER, XW), bf16),
        r2x=pltpu.VMEM((NY, QUARTER, XW), bf16),
        a1y=pltpu.VMEM((NX, QUARTER, YW), f32),
        b2y=pltpu.VMEM((NX, QUARTER, YW), bf16),
        r2y=pltpu.VMEM((NX, QUARTER, YW), bf16),
        packed=pltpu.VMEM((NZ, PAD, XW + YW), f32),
        b3=pltpu.VMEM((NZ, PAD, XW + YW), bf16),
        r3=pltpu.VMEM((NZ, PAD, XW + YW), bf16),
        pz=pltpu.VMEM((NZ, NX, NY, PAD, ZW), f32),
        bz=pltpu.VMEM((NZ, NX, NY, PAD, ZW), bf16),
        rz=pltpu.VMEM((NZ, NX, NY, PAD, ZW), bf16),
        az=pltpu.VMEM((NX, NY, PAD, ZW), f32),
        bzx=pltpu.VMEM((NX, NY, PAD, ZW), bf16),
        rzx=pltpu.VMEM((NX, NY, PAD, ZW), bf16),
        azy=pltpu.VMEM((NY, PAD, ZW), f32),
        bzy=pltpu.VMEM((NY, PAD, ZW), bf16),
        rzy=pltpu.VMEM((NY, PAD, ZW), bf16),
        sent=dma((9,)),
        q0=dma((NX,)),
        q1x=dma,
        q1y=dma((NX,)),
        q2x=dma,
        q2y=dma,
        q3=dma,
        qz=dma((NX,)),
        qzx=dma,
        qzy=dma,
        vc=pltpu.VMEM((2, 8, WIDTH), f32),
        vx=pltpu.VMEM((NX, 8, WIDTH), f32),
        vy=pltpu.VMEM((NY, 8, WIDTH), f32),
        vz=pltpu.VMEM((NZ, 8, WIDTH), f32),
        us=dma((4,)),
        uq=dma((4,)),
    )


class Reducer:
    def __init__(self, g, bufs):
        self.g, self.b = g, bufs
        self.x, self.c, self.y, self.z = coordinates()
        self.piece_xs = ((3,), (2,), (0,), (1,))

    def core_copies(self, piece):
        b = self.b
        return [
            send(
                b.sb.at[xx, 1 - self.c],
                b.r0.at[xx],
                b.sent.at[0],
                b.q0.at[xx],
                at(self.x, 1 - self.c, self.y, self.z),
            )
            for xx in self.piece_xs[piece]
        ]

    def core_start(self, piece):
        for copy in self.core_copies(piece):
            copy.start()

    def round_blocks(self, piece):
        b, g = self.b, self.g
        for xx in self.piece_xs[piece]:

            def body(i, xx=xx):
                b.sb[xx, 1 - self.c, pl.ds(i, 64)] = g[xx, 1 - self.c, pl.ds(i, 64)].astype(jnp.bfloat16)

            chunks(BLOCK, 64, body)

    def first_x(self, xx):
        b = self.b
        return send(
            b.b1.at[xx, :, pl.ds(0, XW)],
            b.r1x.at[self.x],
            b.sent.at[1],
            b.q1x,
            at(xx, self.c, self.y, self.z),
        )

    def first_y(self, piece, k):
        b = self.b
        to = lax.rem(self.y + k, NY)
        xs = self.piece_xs[piece]
        blocks = pl.ds(xs[0], len(xs))
        return send(
            b.b1.at[blocks, pl.ds(pl.multiple_of(to * QUARTER, 16), QUARTER), pl.ds(XW, YW)],
            b.r1y.at[k, blocks],
            b.sent.at[2],
            b.q1y.at[xs[0]],
            at(self.x, self.c, to, self.z),
        )

    def first_start(self, piece):
        b, g = self.b, self.g
        for copy in self.core_copies(piece):
            copy.wait_recv()
        for xx in self.piece_xs[piece]:

            def body(i, xx=xx):
                total = g[xx, self.c, pl.ds(i, 64)] + b.r0[xx, pl.ds(i, 64)].astype(jnp.float32)
                g[xx, self.c, pl.ds(i, 64)] = total
                b.b1[xx, pl.ds(i, 64)] = total.astype(jnp.bfloat16)

            chunks(BLOCK, 64, body)
        for k in (2, 1, 3):
            self.first_y(piece, k).start()
        for xx in self.piece_xs[piece]:

            @pl.when(self.x != xx)
            def _(xx=xx):
                self.first_x(xx).start()

        for xx in self.piece_xs[piece]:

            def group(i, xx=xx):
                yy = i // QUARTER
                part = g[xx, self.c, pl.ds(i, QUARTER), pl.ds(XW + YW, ZW)]
                for zz in range(NZ):
                    rows = part[zz * SHARE : zz * SHARE + SHARE]
                    b.pz[zz, xx, yy, pl.ds(0, SHARE)] = rows
                    b.bz[zz, xx, yy, pl.ds(0, SHARE)] = rows.astype(jnp.bfloat16)

            chunks(BLOCK, QUARTER, group)
            for k in (4, 3, 5, 2, 6, 1, 7):
                self.first_z(xx, k).start()

    def first_z(self, xx, k):
        b = self.b
        to = lax.rem(self.z + k, NZ)
        return send(b.bz.at[to, xx], b.rz.at[k, xx], b.sent.at[6], b.qz.at[xx], at(self.x, self.c, self.y, to))

    def second_z(self, xx):
        b = self.b
        return send(b.bzx.at[xx], b.rzx.at[self.x], b.sent.at[7], b.qzx, at(xx, self.c, self.y, self.z))

    def second_z_start(self, piece):
        b = self.b
        for xx in self.piece_xs[piece]:
            waiter(b.rz.at[pl.ds(1, NZ - 1), xx], b.qz.at[xx]).wait_recv()
            total = b.pz[self.z, xx]
            for k in range(1, NZ):
                total += b.rz[k, xx].astype(jnp.float32)
            b.az[xx] = total
            b.bzx[xx] = total.astype(jnp.bfloat16)

            @pl.when(self.x != xx)
            def _(xx=xx):
                self.second_z(xx).start()

    def third_z(self, k):
        b = self.b
        to = lax.rem(self.y + k, NY)
        return send(b.bzy.at[to], b.rzy.at[k], b.sent.at[8], b.qzy, at(self.x, self.c, to, self.z))

    def third_z_start(self):
        b = self.b
        waiter(b.rzx.at[pl.ds(0, NX - 1)], b.qzx).wait_recv()
        total = b.az[self.x]
        for k in range(1, NX):
            total += b.rzx[lax.rem(self.x + k, NX)].astype(jnp.float32)
        b.azy[...] = total
        b.bzy[...] = total.astype(jnp.bfloat16)
        for k in (2, 1, 3):
            self.third_z(k).start()

    def second_x(self, k):
        b = self.b
        to = lax.rem(self.y + k, NY)
        return send(
            b.b2x.at[to],
            b.r2x.at[k],
            b.sent.at[3],
            b.q2x,
            at(self.x, self.c, to, self.z),
        )

    def second_y(self, xx):
        b = self.b
        return send(
            b.b2y.at[xx],
            b.r2y.at[self.x],
            b.sent.at[4],
            b.q2y,
            at(xx, self.c, self.y, self.z),
        )

    def second_y_start(self, piece):
        b, g = self.b, self.g
        for xx in self.piece_xs[piece]:
            waiter(b.r1y.at[pl.ds(1, NY - 1), xx], b.q1y.at[xx]).wait_recv()
        base = self.y * QUARTER
        for xx in self.piece_xs[piece]:

            def body(i, xx=xx):
                total = g[xx, self.c, pl.ds(pl.multiple_of(base + i, 16), 16), pl.ds(XW, YW)]
                for k in range(1, NY):
                    total += b.r1y[k, xx, pl.ds(i, 16)].astype(jnp.float32)
                b.a1y[xx, pl.ds(i, 16)] = total
                b.b2y[xx, pl.ds(i, 16)] = total.astype(jnp.bfloat16)

            chunks(QUARTER, 16, body)
        for xx in self.piece_xs[piece]:

            @pl.when(self.x != xx)
            def _(xx=xx):
                self.second_y(xx).start()

    def second_x_start(self):
        b, g = self.b, self.g
        waiter(b.r1x.at[pl.ds(0, NX - 1)], b.q1x).wait_recv()
        for yy in range(NY):

            def body(i, yy=yy):
                total = g[self.x, self.c, pl.ds(yy * QUARTER + i, 16), pl.ds(0, XW)]
                for k in range(1, NX):
                    source = lax.rem(self.x + k, NX)
                    total += b.r1x[source, pl.ds(yy * QUARTER + i, 16)].astype(jnp.float32)
                b.a1x[yy, pl.ds(i, 16)] = total
                b.b2x[yy, pl.ds(i, 16)] = total.astype(jnp.bfloat16)

            chunks(QUARTER, 16, body)
        for k in (2, 1, 3):
            self.second_x(k).start()

    def third(self, k):
        b = self.b
        to = lax.rem(self.z + k, NZ)
        return send(
            b.b3.at[to],
            b.r3.at[k],
            b.sent.at[5],
            b.q3,
            at(self.x, self.c, self.y, to),
        )

    def third_start(self):
        b = self.b
        waiter(b.r2x.at[pl.ds(1, NY - 1)], b.q2x).wait_recv()
        waiter(b.r2y.at[pl.ds(0, NX - 1)], b.q2y).wait_recv()
        for i in range(NZ):
            rows = pl.ds(i * SHARE, SHARE)
            left = b.a1x[self.y, rows]
            right = b.a1y[self.x, rows]
            for k in range(1, NY):
                left += b.r2x[k, rows].astype(jnp.float32)
                right += b.r2y[lax.rem(self.x + k, NX), rows].astype(jnp.float32)
            both = jnp.concatenate([left, right], axis=1)
            b.packed[i, pl.ds(0, SHARE)] = both
            b.b3[i, pl.ds(0, SHARE)] = both.astype(jnp.bfloat16)
        for k in (4, 3, 5, 2, 6, 1, 7):
            self.third(k).start()

    def finish(self, out):
        b = self.b
        waiter(b.r3.at[pl.ds(1, NZ - 1)], b.q3).wait_recv()
        total = b.packed[self.z, pl.ds(0, SHARE)]
        for k in range(1, NZ):
            total += b.r3[k, pl.ds(0, SHARE)].astype(jnp.float32)
        for j in range(3):
            out[pl.ds(j, SHARE, stride=4), :] = total[:, 128 * j : 128 * j + 128]
        waiter(b.rzy.at[pl.ds(1, NY - 1)], b.qzy).wait_recv()
        last = b.azy[self.y, pl.ds(0, SHARE)]
        for k in range(1, NY):
            last += b.rzy[k, pl.ds(0, SHARE)].astype(jnp.float32)
        out[pl.ds(3, SHARE, stride=4), :] = last

    def drain(self):
        b = self.b
        for i, ref in enumerate(
            (
                b.r0,
                b.r1x.at[pl.ds(0, NX - 1)],
                b.r1y.at[pl.ds(1, NY - 1)],
                b.r2x.at[pl.ds(1, NY - 1)],
                b.r2y.at[pl.ds(0, NX - 1)],
                b.r3.at[pl.ds(1, NZ - 1)],
                b.rz.at[pl.ds(1, NZ - 1)],
                b.rzx.at[pl.ds(0, NX - 1)],
                b.rzy.at[pl.ds(1, NY - 1)],
            )
        ):
            waiter(ref, b.sent.at[i]).wait_send()

    def vector_copies(self, stage):
        b = self.b
        x, c, y, z = self.x, self.c, self.y, self.z
        if stage == 0:
            return [send(b.vc.at[0], b.vc.at[1], b.us.at[0], b.uq.at[0], at(x, 1 - c, y, z))]
        buf, count, me = ((b.vx, NX, x), (b.vy, NY, y), (b.vz, NZ, z))[stage - 1]
        found = []
        for k in range(1, count):
            to = lax.rem(me + k, count)
            device = (at(to, c, y, z), at(x, c, to, z), at(x, c, y, to))[stage - 1]
            found.append(send(buf.at[me], buf.at[me], b.us.at[stage], b.uq.at[stage], device))
        return found

    def vector_bytes(self, stage):
        b = self.b
        if stage == 0:
            return b.vc.at[1]
        buf, count = ((b.vx, NX), (b.vy, NY), (b.vz, NZ))[stage - 1]
        return buf.at[pl.ds(0, count - 1)]

    def vector_start(self, stage, value=None):
        b = self.b
        if stage > 0:
            (b.vx, b.vy, b.vz)[stage - 1][(self.x, self.y, self.z)[stage - 1]] = value
        for copy in self.vector_copies(stage):
            copy.start()

    def vector_value(self, stage):
        b = self.b
        waiter(self.vector_bytes(stage), b.uq.at[stage]).wait_recv()
        if stage == 0:
            return b.vc[0] + b.vc[1]
        buf = (b.vx, b.vy, b.vz)[stage - 1]
        total = buf[0]
        for i in range(1, buf.shape[0]):
            total += buf[i]
        return total

    def vector_drain(self):
        for stage in range(4):
            waiter(self.vector_bytes(stage), self.b.us.at[stage]).wait_send()


NODES, EDGES, SLOTS, LOOKUP, PICKS = 256, 1024, 32, 320, 640
TILE = 512


def dot(left, right):
    return jnp.dot(left, right, preferred_element_type=jnp.float32)


def dot_nt(left, right):
    return lax.dot_general(left, right, (((1,), (1,)), ((), ())), preferred_element_type=jnp.float32)


def dot_tn(left, right):
    return lax.dot_general(left, right, (((0,), (0,)), ((), ())), preferred_element_type=jnp.float32)


def layer_norm(values):
    centred = values - jnp.mean(values, axis=-1, keepdims=True)
    invstd = lax.rsqrt(jnp.mean(centred * centred, axis=-1, keepdims=True) + 1e-05)
    return centred * invstd, invstd


def norm_back(upstream, normed, invstd, gains):
    scaled = upstream * gains
    return invstd * (
        scaled
        - jnp.mean(scaled, axis=-1, keepdims=True)
        - normed * jnp.mean(scaled * normed, axis=-1, keepdims=True)
    )


def silu_parts(preact):
    sigmoid = 1.0 / (1.0 + jnp.exp(-preact))
    hidden = preact * sigmoid
    return hidden, sigmoid + hidden * (1.0 - sigmoid)


def column_sums(values):
    return jnp.sum(values.reshape(-1, 8, WIDTH), axis=0)


def operands_named(
    nodes, edges, ncot, ecot, wei, weo, wni, wno, eshift, eoff, egain, nshift, noff, ngain, sendid, sndid, rcvid
):
    return SimpleNamespace(**locals())


SMALL = ("eshift", "eoff", "egain", "nshift", "noff", "ngain", "sendid", "sndid", "rcvid")


def compute_scratch():
    bf16, f32 = jnp.bfloat16, jnp.float32
    vm, dma = pltpu.VMEM, pltpu.SemaphoreType.DMA
    return dict(
        g=vm((NX, NC, BLOCK, WIDTH), f32),
        look=vm((LOOKUP, WIDTH), bf16),
        edges_v=vm((EDGES, WIDTH), bf16),
        ncot_v=vm((NODES, WIDTH), bf16),
        ecot_v=vm((EDGES, WIDTH), bf16),
        wei_v=vm((3 * WIDTH, WIDTH), bf16),
        weo_v=vm((WIDTH, WIDTH), bf16),
        wni_v=vm((2 * WIDTH, WIDTH), bf16),
        wno_v=vm((WIDTH, WIDTH), bf16),
        eshift_v=vm((1, WIDTH), f32),
        eoff_v=vm((1, WIDTH), f32),
        egain_v=vm((1, WIDTH), f32),
        nshift_v=vm((1, WIDTH), f32),
        noff_v=vm((1, WIDTH), f32),
        ngain_v=vm((1, WIDTH), f32),
        sendid_v=vm((2, SLOTS), jnp.int32),
        sndid_v=vm((EDGES // 128, 128), jnp.int32),
        rcvid_v=vm((EDGES // 128, 128), jnp.int32),
        loads=dma((18,)),
        pick=vm((EDGES, PICKS), bf16),
        pick_t=vm((PICKS, EDGES), bf16),
        proj=vm((PICKS, WIDTH), bf16),
        outgoing=vm((2 * SLOTS, WIDTH), bf16),
        pre=vm((EDGES, WIDTH), f32),
        dact=vm((EDGES, WIDTH), f32),
        hidden=vm((EDGES, WIDTH), bf16),
        normed=vm((EDGES, WIDTH), f32),
        invstd=vm((EDGES, 128), f32),
        agg=vm((NODES, WIDTH), f32),
        agg_b=vm((NODES, WIDTH), bf16),
        back_b=vm((NODES, WIDTH), bf16),
        nhid=vm((NODES, WIDTH), bf16),
        lhalf=vm((NODES, WIDTH), bf16),
        phalf=vm((NODES, WIDTH), bf16),
        elhalf=vm((EDGES, WIDTH), bf16),
        ephalf=vm((EDGES, WIDTH), bf16),
        gathered=vm((PICKS, WIDTH), bf16),
        rim=vm((2 * SLOTS, WIDTH), bf16),
        back=vm((2 * SLOTS, WIDTH), bf16),
        gnodes=vm((NODES, WIDTH), f32),
        sums=vm((3, 8, WIDTH), f32),
        hs=dma((4,)),
        hq=dma((4,)),
    )


def layer(edge_norm, node_norm, *operands):
    names = list(compute_scratch())
    comm_names = list(reduce_scratch())

    def kernel(*refs):
        given = operands_named(*refs[:17])
        gn_out, ge_out, w_out, v_out = refs[17:21]
        s = SimpleNamespace(**dict(zip(names, refs[21 : 21 + len(names)])))
        bufs = SimpleNamespace(**dict(zip(comm_names, refs[21 + len(names) :])))
        bf16, f32 = jnp.bfloat16, jnp.float32
        barrier_signal()
        red = Reducer(s.g, bufs)
        flat = s.g.reshape(NX * NC * BLOCK, WIDTH)
        wei = given.wei
        loads = dict(
            ecot=(given.ecot, s.ecot_v),
            ncot=(given.ncot, s.ncot_v),
            wno=(given.wno, s.wno_v),
            wni=(given.wni, s.wni_v),
            weo=(given.weo, s.weo_v),
            ws=(wei.at[pl.ds(WIDTH, 2 * WIDTH)], s.wei_v.at[pl.ds(WIDTH, 2 * WIDTH)]),
            edges=(given.edges, s.edges_v),
            we=(wei.at[pl.ds(0, WIDTH)], s.wei_v.at[pl.ds(0, WIDTH)]),
            nodes=(given.nodes, s.look.at[pl.ds(0, NODES)]),
        )
        for name in SMALL:
            loads[name] = (getattr(given, name), getattr(s, name + "_v"))
            setattr(given, name, getattr(s, name + "_v"))
        load = {}
        for i, (name, (src, dst)) in enumerate(reversed(loads.items())):
            load[name] = pltpu.make_async_copy(src, dst, s.loads.at[i])
            load[name].start()
        load = SimpleNamespace(**load)
        w_e = s.wei_v.at[pl.ds(0, WIDTH)]
        w_s = s.wei_v.at[pl.ds(WIDTH, WIDTH)]
        w_r = s.wei_v.at[pl.ds(2 * WIDTH, WIDTH)]
        w_n1 = s.wni_v.at[pl.ds(0, WIDTH)]
        w_n2 = s.wni_v.at[pl.ds(WIDTH, WIDTH)]
        own = s.look.at[pl.ds(0, NODES)]

        for name in SMALL:
            getattr(load, name).wait()

        def one(mask):
            return jnp.where(mask, 1.0, 0.0).astype(bf16)

        send_ids = jnp.concatenate([given.sendid[0:1, :], given.sendid[1:2, :]], axis=1)
        send_t = one(lax.broadcasted_iota(jnp.int32, (NODES, 2 * SLOTS), 0) == send_ids)
        s.proj[pl.ds(NODES + LOOKUP, 64)] = jnp.zeros((64, WIDTH), bf16)

        load.nodes.wait()
        s.outgoing[...] = dot_tn(send_t, own[...]).astype(bf16)
        halo = [
            send(s.outgoing.at[pl.ds(0, SLOTS)], s.look.at[pl.ds(NODES + SLOTS, SLOTS)], s.hs.at[0], s.hq.at[0], beside(-1)),
            send(s.outgoing.at[pl.ds(SLOTS, SLOTS)], s.look.at[pl.ds(NODES, SLOTS)], s.hs.at[1], s.hq.at[1], beside(1)),
        ]
        barrier_wait()
        for copy in halo:
            copy.start()

        for j in range(EDGES // 128):
            lanes = pl.ds(128 * j, 128)
            snd, rcv = given.sndid[j : j + 1, :], given.rcvid[j : j + 1, :]
            s.pick_t[pl.ds(0, NODES), lanes] = one(lax.broadcasted_iota(jnp.int32, (NODES, 128), 0) == rcv)
            s.pick_t[pl.ds(NODES, PICKS - NODES), lanes] = one(
                lax.broadcasted_iota(jnp.int32, (PICKS - NODES, 128), 0) == snd
            )
            snd_c = jnp.broadcast_to(snd, (128, 128)).T
            rcv_c = jnp.broadcast_to(rcv, (128, 128)).T
            lane = lax.broadcasted_iota(jnp.int32, (128, 128), 1)
            for i in range(2):
                s.pick[pl.ds(128 * j, 128), pl.ds(128 * i, 128)] = one(rcv_c == lane + 128 * i)
            for i in range(3):
                s.pick[pl.ds(128 * j, 128), pl.ds(NODES + 128 * i, 128)] = one(snd_c == lane + 128 * i)
        def tiles(body):
            chunks(EDGES, TILE, body)

        load.we.wait()
        load.edges.wait()

        def first(i):
            rows = pl.ds(i, TILE)
            s.pre[rows] = dot(s.edges_v[rows], w_e[...]) + given.eshift[...]

        tiles(first)
        load.ws.wait()
        s.proj[pl.ds(0, NODES)] = dot(own[...], w_r[...]).astype(bf16)
        for copy in halo:
            copy.wait_recv()
        s.proj[pl.ds(NODES, LOOKUP)] = dot(s.look[...], w_s[...]).astype(bf16)
        load.weo.wait()
        s.agg[...] = jnp.zeros((NODES, WIDTH), f32)

        def forward(i):
            rows = pl.ds(i, TILE)
            preact = s.pre[rows] + dot(s.pick[rows], s.proj[...])
            hidden, dact = silu_parts(preact)
            s.dact[rows] = dact
            hidden = hidden.astype(bf16)
            s.hidden[rows] = hidden
            linear = dot(hidden, s.weo_v[...]) + given.eoff[...]
            normed, invstd = layer_norm(linear)
            s.normed[rows] = normed
            s.invstd[rows] = jnp.broadcast_to(invstd, (TILE, 128))
            fresh = (s.edges_v[rows].astype(f32) + given.egain[...] * normed).astype(bf16)
            s.agg[...] += dot(s.pick_t[pl.ds(0, NODES), pl.ds(i, TILE)], fresh)

        tiles(forward)
        load.wni.wait()
        agg = s.agg[...].astype(bf16)
        s.agg_b[...] = agg
        npre = dot(own[...], w_n1[...]) + dot(agg, w_n2[...]) + given.nshift[...]
        nhid, ndact = silu_parts(npre)
        nhid = nhid.astype(bf16)
        s.nhid[...] = nhid
        load.wno.wait()
        nlinear = dot(nhid, s.wno_v[...]) + given.noff[...]
        nnormed, ninvstd = layer_norm(nlinear)
        load.ncot.wait()
        cotan = s.ncot_v[...].astype(f32)
        lback = norm_back(cotan, nnormed, ninvstd, given.ngain[...])
        lhalf = lback.astype(bf16)
        s.lhalf[...] = lhalf
        pback = dot_nt(lhalf, s.wno_v[...]) * ndact
        phalf = pback.astype(bf16)
        s.phalf[...] = phalf
        s.back_b[...] = dot_nt(phalf, w_n2[...]).astype(bf16)
        for row, values in ((3, pback), (4, lback), (5, cotan * nnormed)):
            total = jnp.sum(column_sums(values), axis=0, keepdims=True) * node_norm
            bufs.vc[0, pl.ds(row, 1)] = total
        bufs.vc[0, pl.ds(6, 2)] = jnp.zeros((2, WIDTH), f32)
        s.sums[...] = jnp.zeros((3, 8, WIDTH), f32)
        load.ecot.wait()

        def upstream(rows):
            return s.ecot_v[rows].astype(f32) + dot(s.pick[rows, pl.ds(0, NODES)], s.back_b[...])

        def backward_one(i):
            rows = pl.ds(i, TILE)
            fresh_back = upstream(rows)
            s.pre[rows] = fresh_back
            normed = s.normed[rows]
            eback = norm_back(fresh_back, normed, s.invstd[rows, pl.ds(0, 1)], given.egain[...])
            s.elhalf[rows] = eback.astype(bf16)
            s.sums[1] += column_sums(eback)
            s.sums[2] += column_sums(fresh_back * normed)
            j = i // TILE * 256
            cols = pl.ds(j if isinstance(j, int) else pl.multiple_of(j, 256), 256)
            flat[pl.ds(2048 + j, 256)] = dot_tn(s.look[pl.ds(0, NODES), cols], s.phalf[...]) * node_norm
            flat[pl.ds(2560 + j, 256)] = dot_tn(s.agg_b[:, cols], s.phalf[...]) * node_norm
            flat[pl.ds(3072 + j, 256)] = dot_tn(s.nhid[:, cols], s.lhalf[...]) * node_norm

        tiles(backward_one)
        red.round_blocks(0)
        red.core_start(0)

        def grow(left, right, row, scale, count=2):
            def body(j):
                cols = pl.ds(pl.multiple_of(j, 256), 256)
                flat[pl.ds(pl.multiple_of(row + j, 64), 256)] = dot_tn(left[:, cols], right[...]) * scale

            chunks(256 * count, 256, body)

        grow(s.hidden, s.elhalf, 1536, edge_norm)
        red.first_start(0)
        red.round_blocks(1)
        red.core_start(1)

        def backward_two(i):
            rows = pl.ds(i, TILE)
            epback = dot_nt(s.elhalf[rows], s.weo_v[...]) * s.dact[rows]
            s.ephalf[rows] = epback.astype(bf16)
            s.sums[0] += column_sums(epback)

        tiles(backward_two)
        for row in range(3):
            bufs.vc[0, pl.ds(row, 1)] = jnp.sum(s.sums[row], axis=0, keepdims=True) * edge_norm
        red.vector_start(0)
        red.first_start(1)
        grow(s.edges_v, s.ephalf, 0, edge_norm)

        live = pl.ds(0, NODES + LOOKUP)
        s.gathered[live] = dot(s.pick_t[live], s.ephalf[...]).astype(bf16)
        r_rows, s_rows = pl.ds(0, NODES), pl.ds(NODES, LOOKUP)
        grow(s.look, s.gathered.at[s_rows], 512, edge_norm)
        red.round_blocks(2)
        red.core_start(2)
        grow(s.look.at[r_rows], s.gathered.at[r_rows], 1024, edge_norm)
        red.round_blocks(3)
        red.core_start(3)
        s.rim[...] = dot_nt(s.gathered[pl.ds(2 * NODES, 2 * SLOTS)], w_s[...]).astype(bf16)
        rims = [
            send(s.rim.at[pl.ds(0, SLOTS)], s.back.at[pl.ds(SLOTS, SLOTS)], s.hs.at[2], s.hq.at[2], beside(-1)),
            send(s.rim.at[pl.ds(SLOTS, SLOTS)], s.back.at[pl.ds(0, SLOTS)], s.hs.at[3], s.hq.at[3], beside(1)),
        ]
        for copy in rims:
            copy.start()
        red.vector_start(1, red.vector_value(0))

        def edge_grads(i):
            rows = pl.ds(i, TILE)
            ge_out[rows] = (s.pre[rows] + dot_nt(s.ephalf[rows], w_e[...])).astype(bf16)

        red.first_start(2)
        red.first_start(3)
        red.vector_start(2, red.vector_value(1))
        for piece in range(2):
            red.second_y_start(piece)
            red.second_z_start(piece)
        edge_grads(0)
        edge_grads(TILE)
        s.gnodes[...] = (
            s.ncot_v[...].astype(f32)
            + dot_nt(s.phalf[...], w_n1[...])
            + dot_nt(s.gathered[r_rows], w_r[...])
            + dot_nt(s.gathered[pl.ds(NODES, NODES)], w_s[...])
        )
        for copy in rims:
            copy.wait_recv()
        gn_out[...] = s.gnodes[...] + dot(send_t, s.back[...])
        red.second_y_start(2)
        red.second_z_start(2)
        red.second_y_start(3)
        red.second_z_start(3)
        red.second_x_start()
        red.third_z_start()
        red.vector_start(3, red.vector_value(2))
        red.third_start()
        sums = red.vector_value(3)
        for j in range(WIDTH // 128):
            v_out[pl.ds(j, 6, stride=WIDTH // 128), :] = sums[0:6, 128 * j : 128 * j + 128]
        red.finish(w_out)
        red.drain()
        red.vector_drain()
        for copy in halo + rims:
            copy.wait_send()

    hbm_spec = pl.BlockSpec(memory_space=pltpu.HBM)
    vmem_spec = pl.BlockSpec(memory_space=pltpu.VMEM)
    return pl.pallas_call(
        kernel,
        out_shape=(
            jax.ShapeDtypeStruct((NODES, WIDTH), jnp.float32),
            jax.ShapeDtypeStruct((EDGES, WIDTH), jnp.bfloat16),
            jax.ShapeDtypeStruct((SHARE * WIDTH // 128, 128), jnp.float32),
            jax.ShapeDtypeStruct((6 * WIDTH // 128, 128), jnp.float32),
        ),
        in_specs=[hbm_spec] * 17,
        out_specs=(vmem_spec, vmem_spec, vmem_spec, vmem_spec),
        scratch_shapes=[*compute_scratch().values(), *reduce_scratch().values()],
        compiler_params=pltpu.CompilerParams(
            collective_id=0, has_side_effects=True, vmem_limit_bytes=60 * 1024 * 1024
        ),
        name="layer_back",
    )(*operands)


def store(*values):
    count = len(values)

    def kernel(*refs):
        sems = refs[2 * count]
        copies = [pltpu.make_async_copy(refs[i], refs[count + i], sems.at[i]) for i in range(count)]
        for copy in copies:
            copy.start()
        for copy in copies:
            copy.wait()

    return pl.pallas_call(
        kernel,
        out_shape=tuple(jax.ShapeDtypeStruct(value.shape, value.dtype) for value in values),
        in_specs=[pl.BlockSpec(memory_space=pltpu.VMEM)] * count,
        out_specs=(pl.BlockSpec(memory_space=pltpu.HBM),) * count,
        scratch_shapes=[pltpu.SemaphoreType.DMA((count,))],
        name="store",
    )(*values)


def per_device(
    nodes,
    edges,
    node_cotan,
    edge_cotan,
    edge_inner,
    edge_outer,
    node_inner,
    node_outer,
    edge_shift,
    edge_offset,
    edge_gain,
    node_shift,
    node_offset,
    node_gain,
    send_rows,
    senders,
    receivers,
):
    devices_all = lax.axis_size("region") * lax.axis_size("patch")
    edge_norm = 1.0 / math.sqrt(EDGES * devices_all)
    node_norm = 1.0 / math.sqrt(NODES * devices_all)
    vectors = (edge_shift, edge_offset, edge_gain, node_shift, node_offset, node_gain)
    grad_nodes, grad_edges, weights, vector_sums = layer(
        edge_norm,
        node_norm,
        nodes,
        edges,
        node_cotan,
        edge_cotan,
        edge_inner,
        edge_outer,
        node_inner,
        node_outer,
        *(vector.reshape(1, WIDTH) for vector in vectors),
        send_rows.reshape(2, SLOTS),
        senders.reshape(EDGES // 128, 128),
        receivers.reshape(EDGES // 128, 128),
    )
    grad_nodes, grad_edges, weights, vector_sums = store(grad_nodes, grad_edges, weights, vector_sums)
    return (grad_nodes, grad_edges, weights.reshape(-1), vector_sums.reshape(-1))


def solution(mesh):
    in_specs = (
        P(("region", "patch"), None),
        P(("region", "patch"), None),
        P(("region", "patch"), None),
        P(("region", "patch"), None),
        P(),
        P(),
        P(),
        P(),
        P(),
        P(),
        P(),
        P(),
        P(),
        P(),
        P("region", "patch", None, None),
        P(("region", "patch")),
        P(("region", "patch")),
    )
    out_specs = (
        P(("region", "patch"), None),
        P(("region", "patch"), None),
        P(("region", "patch")),
        P(),
    )
    return jax.shard_map(
        per_device, mesh=mesh, in_specs=in_specs, out_specs=out_specs, check_vma=False
    )
```

```python
import math
from types import SimpleNamespace

import jax
import jax.numpy as jnp
from jax import lax
from jax.experimental import pallas as pl
from jax.experimental.pallas import tpu as pltpu
from jax.sharding import PartitionSpec as P

MESH = pl.DeviceIdType.MESH
NX, NC, NY, NZ = 4, 2, 4, 8
WIDTH, XW, YW, ZW = 512, 128, 256, 128
BLOCK, QUARTER, SHARE, PAD = 448, 112, 14, 16


def coordinates():
    region, patch = lax.axis_index("region"), lax.axis_index("patch")
    return region // NC, lax.rem(region, NC), patch // NZ, lax.rem(patch, NZ)


def at(x, c, y, z):
    return (x * NC + c, y * NZ + z)


def beside(step):
    region, patch = lax.axis_index("region"), lax.axis_index("patch")
    return (region, lax.rem(patch + step + NY * NZ, NY * NZ))


def peers():
    x, c, y, z = coordinates()
    found = [at(x, 1 - c, y, z), beside(1), beside(-1)]
    found += [at(lax.rem(x + k, NX), c, y, z) for k in range(1, NX)]
    found += [at(x, c, lax.rem(y + k, NY), z) for k in range(1, NY)]
    found += [at(x, c, y, lax.rem(z + k, NZ)) for k in range(1, NZ)]
    return found


def barrier_signal():
    barrier = pltpu.get_barrier_semaphore()
    for device in peers():
        pl.semaphore_signal(barrier, inc=1, device_id=device, device_id_type=MESH)


def barrier_wait():
    pl.semaphore_wait(pltpu.get_barrier_semaphore(), len(peers()))


def send(src, dst, send_sem, recv_sem, device):
    return pltpu.make_async_remote_copy(
        src_ref=src,
        dst_ref=dst,
        send_sem=send_sem,
        recv_sem=recv_sem,
        device_id=device,
        device_id_type=MESH,
    )


def waiter(ref, sem):
    x, c, y, z = coordinates()
    return send(ref, ref, sem, sem, at(x, 1 - c, y, z))


def chunks(total, step, body):
    def one(i, carry):
        body(pl.multiple_of(i * step, step))
        return carry

    lax.fori_loop(0, total // step, one, 0)


def reduce_scratch():
    bf16, f32 = jnp.bfloat16, jnp.float32
    dma = pltpu.SemaphoreType.DMA
    return dict(
        sb=pltpu.VMEM((NX, NC, BLOCK, WIDTH), bf16),
        r0=pltpu.VMEM((NX, BLOCK, WIDTH), bf16),
        b1=pltpu.VMEM((NX, BLOCK, WIDTH), bf16),
        r1x=pltpu.VMEM((NX, BLOCK, XW), bf16),
        r1y=pltpu.VMEM((NY, NX, QUARTER, YW), bf16),
        a1x=pltpu.VMEM((NY, QUARTER, XW), f32),
        b2x=pltpu.VMEM((NY, QUARTER, XW), bf16),
        r2x=pltpu.VMEM((NY, QUARTER, XW), bf16),
        a1y=pltpu.VMEM((NX, QUARTER, YW), f32),
        b2y=pltpu.VMEM((NX, QUARTER, YW), bf16),
        r2y=pltpu.VMEM((NX, QUARTER, YW), bf16),
        packed=pltpu.VMEM((NZ, PAD, XW + YW), f32),
        b3=pltpu.VMEM((NZ, PAD, XW + YW), bf16),
        r3=pltpu.VMEM((NZ, PAD, XW + YW), bf16),
        pz=pltpu.VMEM((NZ, NX, NY, PAD, ZW), f32),
        bz=pltpu.VMEM((NZ, NX, NY, PAD, ZW), bf16),
        rz=pltpu.VMEM((NZ, NX, NY, PAD, ZW), bf16),
        az=pltpu.VMEM((NX, NY, PAD, ZW), f32),
        bzx=pltpu.VMEM((NX, NY, PAD, ZW), bf16),
        rzx=pltpu.VMEM((NX, NY, PAD, ZW), bf16),
        azy=pltpu.VMEM((NY, PAD, ZW), f32),
        bzy=pltpu.VMEM((NY, PAD, ZW), bf16),
        rzy=pltpu.VMEM((NY, PAD, ZW), bf16),
        sent=dma((9,)),
        q0=dma((NX,)),
        q1x=dma,
        q1y=dma((NX,)),
        q2x=dma,
        q2y=dma,
        q3=dma,
        qz=dma((NX,)),
        qzx=dma,
        qzy=dma,
        vc=pltpu.VMEM((2, 8, WIDTH), f32),
        vx=pltpu.VMEM((NX, 8, WIDTH), f32),
        vy=pltpu.VMEM((NY, 8, WIDTH), f32),
        vz=pltpu.VMEM((NZ, 8, WIDTH), f32),
        us=dma((4,)),
        uq=dma((4,)),
    )


class Reducer:
    def __init__(self, g, bufs):
        self.g, self.b = g, bufs
        self.x, self.c, self.y, self.z = coordinates()
        self.piece_xs = ((3,), (2,), (0,), (1,))

    def core_copies(self, piece):
        b = self.b
        return [
            send(
                b.sb.at[xx, 1 - self.c],
                b.r0.at[xx],
                b.sent.at[0],
                b.q0.at[xx],
                at(self.x, 1 - self.c, self.y, self.z),
            )
            for xx in self.piece_xs[piece]
        ]

    def core_start(self, piece):
        for copy in self.core_copies(piece):
            copy.start()

    def round_blocks(self, piece):
        b, g = self.b, self.g
        for xx in self.piece_xs[piece]:

            def body(i, xx=xx):
                b.sb[xx, 1 - self.c, pl.ds(i, 64)] = g[xx, 1 - self.c, pl.ds(i, 64)].astype(jnp.bfloat16)

            chunks(BLOCK, 64, body)

    def first_x(self, xx):
        b = self.b
        return send(
            b.b1.at[xx, :, pl.ds(0, XW)],
            b.r1x.at[self.x],
            b.sent.at[1],
            b.q1x,
            at(xx, self.c, self.y, self.z),
        )

    def first_y(self, piece, k):
        b = self.b
        to = lax.rem(self.y + k, NY)
        xs = self.piece_xs[piece]
        blocks = pl.ds(xs[0], len(xs))
        return send(
            b.b1.at[blocks, pl.ds(pl.multiple_of(to * QUARTER, 16), QUARTER), pl.ds(XW, YW)],
            b.r1y.at[k, blocks],
            b.sent.at[2],
            b.q1y.at[xs[0]],
            at(self.x, self.c, to, self.z),
        )

    def first_start(self, piece):
        b, g = self.b, self.g
        for copy in self.core_copies(piece):
            copy.wait_recv()
        for xx in self.piece_xs[piece]:

            def body(i, xx=xx):
                total = g[xx, self.c, pl.ds(i, 64)] + b.r0[xx, pl.ds(i, 64)].astype(jnp.float32)
                g[xx, self.c, pl.ds(i, 64)] = total
                b.b1[xx, pl.ds(i, 64)] = total.astype(jnp.bfloat16)

            chunks(BLOCK, 64, body)
        for k in (2, 1, 3):
            self.first_y(piece, k).start()
        for xx in self.piece_xs[piece]:

            @pl.when(self.x != xx)
            def _(xx=xx):
                self.first_x(xx).start()

        for xx in self.piece_xs[piece]:

            def group(i, xx=xx):
                yy = i // QUARTER
                part = g[xx, self.c, pl.ds(i, QUARTER), pl.ds(XW + YW, ZW)]
                for zz in range(NZ):
                    rows = part[zz * SHARE : zz * SHARE + SHARE]
                    b.pz[zz, xx, yy, pl.ds(0, SHARE)] = rows
                    b.bz[zz, xx, yy, pl.ds(0, SHARE)] = rows.astype(jnp.bfloat16)

            chunks(BLOCK, QUARTER, group)
            for k in (4, 3, 5, 2, 6, 1, 7):
                self.first_z(xx, k).start()

    def first_z(self, xx, k):
        b = self.b
        to = lax.rem(self.z + k, NZ)
        return send(b.bz.at[to, xx], b.rz.at[k, xx], b.sent.at[6], b.qz.at[xx], at(self.x, self.c, self.y, to))

    def second_z(self, xx):
        b = self.b
        return send(b.bzx.at[xx], b.rzx.at[self.x], b.sent.at[7], b.qzx, at(xx, self.c, self.y, self.z))

    def second_z_start(self, piece):
        b = self.b
        for xx in self.piece_xs[piece]:
            waiter(b.rz.at[pl.ds(1, NZ - 1), xx], b.qz.at[xx]).wait_recv()
            total = b.pz[self.z, xx]
            for k in range(1, NZ):
                total += b.rz[k, xx].astype(jnp.float32)
            b.az[xx] = total
            b.bzx[xx] = total.astype(jnp.bfloat16)

            @pl.when(self.x != xx)
            def _(xx=xx):
                self.second_z(xx).start()

    def third_z(self, k):
        b = self.b
        to = lax.rem(self.y + k, NY)
        return send(b.bzy.at[to], b.rzy.at[k], b.sent.at[8], b.qzy, at(self.x, self.c, to, self.z))

    def third_z_start(self):
        b = self.b
        waiter(b.rzx.at[pl.ds(0, NX - 1)], b.qzx).wait_recv()
        total = b.az[self.x]
        for k in range(1, NX):
            total += b.rzx[lax.rem(self.x + k, NX)].astype(jnp.float32)
        b.azy[...] = total
        b.bzy[...] = total.astype(jnp.bfloat16)
        for k in (2, 1, 3):
            self.third_z(k).start()

    def second_x(self, k):
        b = self.b
        to = lax.rem(self.y + k, NY)
        return send(
            b.b2x.at[to],
            b.r2x.at[k],
            b.sent.at[3],
            b.q2x,
            at(self.x, self.c, to, self.z),
        )

    def second_y(self, xx):
        b = self.b
        return send(
            b.b2y.at[xx],
            b.r2y.at[self.x],
            b.sent.at[4],
            b.q2y,
            at(xx, self.c, self.y, self.z),
        )

    def second_y_start(self, piece):
        b, g = self.b, self.g
        for xx in self.piece_xs[piece]:
            waiter(b.r1y.at[pl.ds(1, NY - 1), xx], b.q1y.at[xx]).wait_recv()
        base = self.y * QUARTER
        for xx in self.piece_xs[piece]:

            def body(i, xx=xx):
                total = g[xx, self.c, pl.ds(pl.multiple_of(base + i, 16), 16), pl.ds(XW, YW)]
                for k in range(1, NY):
                    total += b.r1y[k, xx, pl.ds(i, 16)].astype(jnp.float32)
                b.a1y[xx, pl.ds(i, 16)] = total
                b.b2y[xx, pl.ds(i, 16)] = total.astype(jnp.bfloat16)

            chunks(QUARTER, 16, body)
        for xx in self.piece_xs[piece]:

            @pl.when(self.x != xx)
            def _(xx=xx):
                self.second_y(xx).start()

    def second_x_start(self):
        b, g = self.b, self.g
        waiter(b.r1x.at[pl.ds(0, NX - 1)], b.q1x).wait_recv()
        for yy in range(NY):

            def body(i, yy=yy):
                total = g[self.x, self.c, pl.ds(yy * QUARTER + i, 16), pl.ds(0, XW)]
                for k in range(1, NX):
                    source = lax.rem(self.x + k, NX)
                    total += b.r1x[source, pl.ds(yy * QUARTER + i, 16)].astype(jnp.float32)
                b.a1x[yy, pl.ds(i, 16)] = total
                b.b2x[yy, pl.ds(i, 16)] = total.astype(jnp.bfloat16)

            chunks(QUARTER, 16, body)
        for k in (2, 1, 3):
            self.second_x(k).start()

    def third(self, k):
        b = self.b
        to = lax.rem(self.z + k, NZ)
        return send(
            b.b3.at[to],
            b.r3.at[k],
            b.sent.at[5],
            b.q3,
            at(self.x, self.c, self.y, to),
        )

    def third_start(self):
        b = self.b
        waiter(b.r2x.at[pl.ds(1, NY - 1)], b.q2x).wait_recv()
        waiter(b.r2y.at[pl.ds(0, NX - 1)], b.q2y).wait_recv()
        for i in range(NZ):
            rows = pl.ds(i * SHARE, SHARE)
            left = b.a1x[self.y, rows]
            right = b.a1y[self.x, rows]
            for k in range(1, NY):
                left += b.r2x[k, rows].astype(jnp.float32)
                right += b.r2y[lax.rem(self.x + k, NX), rows].astype(jnp.float32)
            both = jnp.concatenate([left, right], axis=1)
            b.packed[i, pl.ds(0, SHARE)] = both
            b.b3[i, pl.ds(0, SHARE)] = both.astype(jnp.bfloat16)
        for k in (4, 3, 5, 2, 6, 1, 7):
            self.third(k).start()

    def finish(self, out):
        b = self.b
        waiter(b.r3.at[pl.ds(1, NZ - 1)], b.q3).wait_recv()
        total = b.packed[self.z, pl.ds(0, SHARE)]
        for k in range(1, NZ):
            total += b.r3[k, pl.ds(0, SHARE)].astype(jnp.float32)
        for j in range(3):
            out[pl.ds(j, SHARE, stride=4), :] = total[:, 128 * j : 128 * j + 128]
        waiter(b.rzy.at[pl.ds(1, NY - 1)], b.qzy).wait_recv()
        last = b.azy[self.y, pl.ds(0, SHARE)]
        for k in range(1, NY):
            last += b.rzy[k, pl.ds(0, SHARE)].astype(jnp.float32)
        out[pl.ds(3, SHARE, stride=4), :] = last

    def drain(self):
        b = self.b
        for i, ref in enumerate(
            (
                b.r0,
                b.r1x.at[pl.ds(0, NX - 1)],
                b.r1y.at[pl.ds(1, NY - 1)],
                b.r2x.at[pl.ds(1, NY - 1)],
                b.r2y.at[pl.ds(0, NX - 1)],
                b.r3.at[pl.ds(1, NZ - 1)],
                b.rz.at[pl.ds(1, NZ - 1)],
                b.rzx.at[pl.ds(0, NX - 1)],
                b.rzy.at[pl.ds(1, NY - 1)],
            )
        ):
            waiter(ref, b.sent.at[i]).wait_send()

    def vector_copies(self, stage):
        b = self.b
        x, c, y, z = self.x, self.c, self.y, self.z
        if stage == 0:
            return [send(b.vc.at[0], b.vc.at[1], b.us.at[0], b.uq.at[0], at(x, 1 - c, y, z))]
        buf, count, me = ((b.vx, NX, x), (b.vy, NY, y), (b.vz, NZ, z))[stage - 1]
        found = []
        for k in range(1, count):
            to = lax.rem(me + k, count)
            device = (at(to, c, y, z), at(x, c, to, z), at(x, c, y, to))[stage - 1]
            found.append(send(buf.at[me], buf.at[me], b.us.at[stage], b.uq.at[stage], device))
        return found

    def vector_bytes(self, stage):
        b = self.b
        if stage == 0:
            return b.vc.at[1]
        buf, count = ((b.vx, NX), (b.vy, NY), (b.vz, NZ))[stage - 1]
        return buf.at[pl.ds(0, count - 1)]

    def vector_start(self, stage, value=None):
        b = self.b
        if stage > 0:
            (b.vx, b.vy, b.vz)[stage - 1][(self.x, self.y, self.z)[stage - 1]] = value
        for copy in self.vector_copies(stage):
            copy.start()

    def vector_value(self, stage):
        b = self.b
        waiter(self.vector_bytes(stage), b.uq.at[stage]).wait_recv()
        if stage == 0:
            return b.vc[0] + b.vc[1]
        buf = (b.vx, b.vy, b.vz)[stage - 1]
        total = buf[0]
        for i in range(1, buf.shape[0]):
            total += buf[i]
        return total

    def vector_drain(self):
        for stage in range(4):
            waiter(self.vector_bytes(stage), self.b.us.at[stage]).wait_send()


NODES, EDGES, SLOTS, LOOKUP, PICKS = 256, 1024, 32, 320, 640
TILE = 512


def dot(left, right):
    return jnp.dot(left, right, preferred_element_type=jnp.float32)


def dot_nt(left, right):
    return lax.dot_general(left, right, (((1,), (1,)), ((), ())), preferred_element_type=jnp.float32)


def dot_tn(left, right):
    return lax.dot_general(left, right, (((0,), (0,)), ((), ())), preferred_element_type=jnp.float32)


def layer_norm(values):
    centred = values - jnp.mean(values, axis=-1, keepdims=True)
    invstd = lax.rsqrt(jnp.mean(centred * centred, axis=-1, keepdims=True) + 1e-05)
    return centred * invstd, invstd


def norm_back(upstream, normed, invstd, gains):
    scaled = upstream * gains
    return invstd * (
        scaled
        - jnp.mean(scaled, axis=-1, keepdims=True)
        - normed * jnp.mean(scaled * normed, axis=-1, keepdims=True)
    )


def silu_parts(preact):
    sigmoid = 0.5 * jnp.tanh(0.5 * preact) + 0.5
    hidden = preact * sigmoid
    return hidden, sigmoid + hidden * (1.0 - sigmoid)


def column_sums(values):
    return jnp.sum(values.reshape(-1, 8, WIDTH), axis=0)


def operands_named(
    nodes, edges, ncot, ecot, wei, weo, wni, wno, eshift, eoff, egain, nshift, noff, ngain, sendid, sndid, rcvid
):
    return SimpleNamespace(**locals())


SMALL = ("eshift", "eoff", "egain", "nshift", "noff", "ngain", "sendid", "sndid", "rcvid")


def compute_scratch():
    bf16, f32 = jnp.bfloat16, jnp.float32
    vm, dma = pltpu.VMEM, pltpu.SemaphoreType.DMA
    return dict(
        g=vm((NX, NC, BLOCK, WIDTH), f32),
        look=vm((LOOKUP, WIDTH), bf16),
        edges_v=vm((EDGES, WIDTH), bf16),
        ncot_v=vm((NODES, WIDTH), bf16),
        ecot_v=vm((EDGES, WIDTH), bf16),
        wei_v=vm((3 * WIDTH, WIDTH), bf16),
        weo_v=vm((WIDTH, WIDTH), bf16),
        wni_v=vm((2 * WIDTH, WIDTH), bf16),
        wno_v=vm((WIDTH, WIDTH), bf16),
        eshift_v=vm((1, WIDTH), f32),
        eoff_v=vm((1, WIDTH), f32),
        egain_v=vm((1, WIDTH), f32),
        nshift_v=vm((1, WIDTH), f32),
        noff_v=vm((1, WIDTH), f32),
        ngain_v=vm((1, WIDTH), f32),
        sendid_v=vm((2, SLOTS), jnp.int32),
        sndid_v=vm((EDGES // 128, 128), jnp.int32),
        rcvid_v=vm((EDGES // 128, 128), jnp.int32),
        loads=dma((18,)),
        pick=vm((EDGES, PICKS), bf16),
        pick_t=vm((PICKS, EDGES), bf16),
        proj=vm((PICKS, WIDTH), bf16),
        outgoing=vm((2 * SLOTS, WIDTH), bf16),
        pre=vm((EDGES, WIDTH), f32),
        dact=vm((EDGES, WIDTH), f32),
        hidden=vm((EDGES, WIDTH), bf16),
        normed=vm((EDGES, WIDTH), f32),
        invstd=vm((EDGES, 128), f32),
        agg=vm((NODES, WIDTH), f32),
        agg_b=vm((NODES, WIDTH), bf16),
        back_b=vm((NODES, WIDTH), bf16),
        nhid=vm((NODES, WIDTH), bf16),
        lhalf=vm((NODES, WIDTH), bf16),
        phalf=vm((NODES, WIDTH), bf16),
        elhalf=vm((EDGES, WIDTH), bf16),
        ephalf=vm((EDGES, WIDTH), bf16),
        gathered=vm((PICKS, WIDTH), bf16),
        rim=vm((2 * SLOTS, WIDTH), bf16),
        back=vm((2 * SLOTS, WIDTH), bf16),
        gnodes=vm((NODES, WIDTH), f32),
        sums=vm((3, 8, WIDTH), f32),
        hs=dma((4,)),
        hq=dma((4,)),
    )


def layer(edge_norm, node_norm, *operands):
    names = list(compute_scratch())
    comm_names = list(reduce_scratch())

    def kernel(*refs):
        given = operands_named(*refs[:17])
        gn_out, ge_out, w_out, v_out = refs[17:21]
        s = SimpleNamespace(**dict(zip(names, refs[21 : 21 + len(names)])))
        bufs = SimpleNamespace(**dict(zip(comm_names, refs[21 + len(names) :])))
        bf16, f32 = jnp.bfloat16, jnp.float32
        barrier_signal()
        red = Reducer(s.g, bufs)
        flat = s.g.reshape(NX * NC * BLOCK, WIDTH)
        wei = given.wei
        loads = dict(
            ecot=(given.ecot, s.ecot_v),
            ncot=(given.ncot, s.ncot_v),
            wno=(given.wno, s.wno_v),
            wni=(given.wni, s.wni_v),
            weo=(given.weo, s.weo_v),
            ws=(wei.at[pl.ds(WIDTH, 2 * WIDTH)], s.wei_v.at[pl.ds(WIDTH, 2 * WIDTH)]),
            edges=(given.edges, s.edges_v),
            we=(wei.at[pl.ds(0, WIDTH)], s.wei_v.at[pl.ds(0, WIDTH)]),
            nodes=(given.nodes, s.look.at[pl.ds(0, NODES)]),
        )
        for name in SMALL:
            loads[name] = (getattr(given, name), getattr(s, name + "_v"))
            setattr(given, name, getattr(s, name + "_v"))
        load = {}
        for i, (name, (src, dst)) in enumerate(reversed(loads.items())):
            load[name] = pltpu.make_async_copy(src, dst, s.loads.at[i])
            load[name].start()
        load = SimpleNamespace(**load)
        w_e = s.wei_v.at[pl.ds(0, WIDTH)]
        w_s = s.wei_v.at[pl.ds(WIDTH, WIDTH)]
        w_r = s.wei_v.at[pl.ds(2 * WIDTH, WIDTH)]
        w_n1 = s.wni_v.at[pl.ds(0, WIDTH)]
        w_n2 = s.wni_v.at[pl.ds(WIDTH, WIDTH)]
        own = s.look.at[pl.ds(0, NODES)]

        for name in SMALL:
            getattr(load, name).wait()

        def one(mask):
            return jnp.where(mask, 1.0, 0.0).astype(bf16)

        send_ids = jnp.concatenate([given.sendid[0:1, :], given.sendid[1:2, :]], axis=1)
        send_t = one(lax.broadcasted_iota(jnp.int32, (NODES, 2 * SLOTS), 0) == send_ids)
        s.proj[pl.ds(NODES + LOOKUP, 64)] = jnp.zeros((64, WIDTH), bf16)

        load.nodes.wait()
        s.outgoing[...] = dot_tn(send_t, own[...]).astype(bf16)
        halo = [
            send(s.outgoing.at[pl.ds(0, SLOTS)], s.look.at[pl.ds(NODES + SLOTS, SLOTS)], s.hs.at[0], s.hq.at[0], beside(-1)),
            send(s.outgoing.at[pl.ds(SLOTS, SLOTS)], s.look.at[pl.ds(NODES, SLOTS)], s.hs.at[1], s.hq.at[1], beside(1)),
        ]
        barrier_wait()
        for copy in halo:
            copy.start()

        for j in range(EDGES // 128):
            lanes = pl.ds(128 * j, 128)
            snd, rcv = given.sndid[j : j + 1, :], given.rcvid[j : j + 1, :]
            s.pick_t[pl.ds(0, NODES), lanes] = one(lax.broadcasted_iota(jnp.int32, (NODES, 128), 0) == rcv)
            s.pick_t[pl.ds(NODES, PICKS - NODES), lanes] = one(
                lax.broadcasted_iota(jnp.int32, (PICKS - NODES, 128), 0) == snd
            )
            snd_c = jnp.broadcast_to(snd, (128, 128)).T
            rcv_c = jnp.broadcast_to(rcv, (128, 128)).T
            lane = lax.broadcasted_iota(jnp.int32, (128, 128), 1)
            for i in range(2):
                s.pick[pl.ds(128 * j, 128), pl.ds(128 * i, 128)] = one(rcv_c == lane + 128 * i)
            for i in range(3):
                s.pick[pl.ds(128 * j, 128), pl.ds(NODES + 128 * i, 128)] = one(snd_c == lane + 128 * i)
        def tiles(body):
            for i in range(0, EDGES, TILE):
                body(i)

        load.we.wait()
        load.edges.wait()

        def first(i):
            rows = pl.ds(i, TILE)
            s.pre[rows] = dot(s.edges_v[rows], w_e[...]) + given.eshift[...]

        tiles(first)
        load.ws.wait()
        s.proj[pl.ds(0, NODES)] = dot(own[...], w_r[...]).astype(bf16)
        for copy in halo:
            copy.wait_recv()
        s.proj[pl.ds(NODES, LOOKUP)] = dot(s.look[...], w_s[...]).astype(bf16)
        load.weo.wait()
        s.agg[...] = jnp.zeros((NODES, WIDTH), f32)

        def forward(i):
            rows = pl.ds(i, TILE)
            preact = s.pre[rows] + dot(s.pick[rows], s.proj[...])
            hidden, dact = silu_parts(preact)
            s.dact[rows] = dact
            hidden = hidden.astype(bf16)
            s.hidden[rows] = hidden
            linear = dot(hidden, s.weo_v[...]) + given.eoff[...]
            normed, invstd = layer_norm(linear)
            s.normed[rows] = normed
            s.invstd[rows] = jnp.broadcast_to(invstd, (TILE, 128))
            fresh = (s.edges_v[rows].astype(f32) + given.egain[...] * normed).astype(bf16)
            s.agg[...] += dot(s.pick_t[pl.ds(0, NODES), pl.ds(i, TILE)], fresh)

        tiles(forward)
        load.wni.wait()
        agg = s.agg[...].astype(bf16)
        s.agg_b[...] = agg
        npre = dot(own[...], w_n1[...]) + dot(agg, w_n2[...]) + given.nshift[...]
        nhid, ndact = silu_parts(npre)
        nhid = nhid.astype(bf16)
        s.nhid[...] = nhid
        load.wno.wait()
        nlinear = dot(nhid, s.wno_v[...]) + given.noff[...]
        nnormed, ninvstd = layer_norm(nlinear)
        load.ncot.wait()
        cotan = s.ncot_v[...].astype(f32)
        lback = norm_back(cotan, nnormed, ninvstd, given.ngain[...])
        lhalf = lback.astype(bf16)
        s.lhalf[...] = lhalf
        pback = dot_nt(lhalf, s.wno_v[...]) * ndact
        phalf = pback.astype(bf16)
        s.phalf[...] = phalf
        s.back_b[...] = dot_nt(phalf, w_n2[...]).astype(bf16)
        for row, values in ((3, pback), (4, lback), (5, cotan * nnormed)):
            total = jnp.sum(column_sums(values), axis=0, keepdims=True) * node_norm
            bufs.vc[0, pl.ds(row, 1)] = total
        bufs.vc[0, pl.ds(6, 2)] = jnp.zeros((2, WIDTH), f32)
        s.sums[...] = jnp.zeros((3, 8, WIDTH), f32)
        load.ecot.wait()

        def upstream(rows):
            return s.ecot_v[rows].astype(f32) + dot(s.pick[rows, pl.ds(0, NODES)], s.back_b[...])

        def backward_one(i):
            rows = pl.ds(i, TILE)
            fresh_back = upstream(rows)
            s.pre[rows] = fresh_back
            normed = s.normed[rows]
            eback = norm_back(fresh_back, normed, s.invstd[rows, pl.ds(0, 1)], given.egain[...])
            s.elhalf[rows] = eback.astype(bf16)
            s.sums[1] += column_sums(eback)
            s.sums[2] += column_sums(fresh_back * normed)
            j = i // TILE * 256
            cols = pl.ds(j if isinstance(j, int) else pl.multiple_of(j, 256), 256)
            flat[pl.ds(2048 + j, 256)] = dot_tn(s.look[pl.ds(0, NODES), cols], s.phalf[...]) * node_norm
            flat[pl.ds(2560 + j, 256)] = dot_tn(s.agg_b[:, cols], s.phalf[...]) * node_norm
            flat[pl.ds(3072 + j, 256)] = dot_tn(s.nhid[:, cols], s.lhalf[...]) * node_norm

        tiles(backward_one)
        red.round_blocks(0)
        red.core_start(0)

        def grow(left, right, row, scale, count=2):
            def body(j):
                cols = pl.ds(pl.multiple_of(j, 256), 256)
                flat[pl.ds(pl.multiple_of(row + j, 64), 256)] = dot_tn(left[:, cols], right[...]) * scale

            chunks(256 * count, 256, body)

        grow(s.hidden, s.elhalf, 1536, edge_norm)
        red.first_start(0)
        red.round_blocks(1)
        red.core_start(1)

        def backward_two(i):
            rows = pl.ds(i, TILE)
            epback = dot_nt(s.elhalf[rows], s.weo_v[...]) * s.dact[rows]
            s.ephalf[rows] = epback.astype(bf16)
            s.sums[0] += column_sums(epback)

        tiles(backward_two)
        for row in range(3):
            bufs.vc[0, pl.ds(row, 1)] = jnp.sum(s.sums[row], axis=0, keepdims=True) * edge_norm
        red.vector_start(0)
        red.first_start(1)
        grow(s.edges_v, s.ephalf, 0, edge_norm)

        live = pl.ds(0, NODES + LOOKUP)
        s.gathered[live] = dot(s.pick_t[live], s.ephalf[...]).astype(bf16)
        r_rows, s_rows = pl.ds(0, NODES), pl.ds(NODES, LOOKUP)
        grow(s.look, s.gathered.at[s_rows], 512, edge_norm)
        red.round_blocks(2)
        red.core_start(2)
        grow(s.look.at[r_rows], s.gathered.at[r_rows], 1024, edge_norm)
        red.round_blocks(3)
        red.core_start(3)
        s.rim[...] = dot_nt(s.gathered[pl.ds(2 * NODES, 2 * SLOTS)], w_s[...]).astype(bf16)
        rims = [
            send(s.rim.at[pl.ds(0, SLOTS)], s.back.at[pl.ds(SLOTS, SLOTS)], s.hs.at[2], s.hq.at[2], beside(-1)),
            send(s.rim.at[pl.ds(SLOTS, SLOTS)], s.back.at[pl.ds(0, SLOTS)], s.hs.at[3], s.hq.at[3], beside(1)),
        ]
        for copy in rims:
            copy.start()
        red.vector_start(1, red.vector_value(0))

        def edge_grads(i):
            rows = pl.ds(i, TILE)
            ge_out[rows] = (s.pre[rows] + dot_nt(s.ephalf[rows], w_e[...])).astype(bf16)

        red.first_start(2)
        red.first_start(3)
        red.vector_start(2, red.vector_value(1))
        for piece in range(2):
            red.second_y_start(piece)
            red.second_z_start(piece)
        edge_grads(0)
        edge_grads(TILE)
        s.gnodes[...] = (
            s.ncot_v[...].astype(f32)
            + dot_nt(s.phalf[...], w_n1[...])
            + dot_nt(s.gathered[r_rows], w_r[...])
            + dot_nt(s.gathered[pl.ds(NODES, NODES)], w_s[...])
        )
        for copy in rims:
            copy.wait_recv()
        gn_out[...] = s.gnodes[...] + dot(send_t, s.back[...])
        red.second_y_start(2)
        red.second_z_start(2)
        red.second_y_start(3)
        red.second_z_start(3)
        red.second_x_start()
        red.third_z_start()
        red.vector_start(3, red.vector_value(2))
        red.third_start()
        sums = red.vector_value(3)
        for j in range(WIDTH // 128):
            v_out[pl.ds(j, 6, stride=WIDTH // 128), :] = sums[0:6, 128 * j : 128 * j + 128]
        red.finish(w_out)
        red.drain()
        red.vector_drain()
        for copy in halo + rims:
            copy.wait_send()

    hbm_spec = pl.BlockSpec(memory_space=pltpu.HBM)
    vmem_spec = pl.BlockSpec(memory_space=pltpu.VMEM)
    return pl.pallas_call(
        kernel,
        out_shape=(
            jax.ShapeDtypeStruct((NODES, WIDTH), jnp.float32),
            jax.ShapeDtypeStruct((EDGES, WIDTH), jnp.bfloat16),
            jax.ShapeDtypeStruct((SHARE * WIDTH // 128, 128), jnp.float32),
            jax.ShapeDtypeStruct((6 * WIDTH // 128, 128), jnp.float32),
        ),
        in_specs=[hbm_spec] * 17,
        out_specs=(vmem_spec, vmem_spec, vmem_spec, vmem_spec),
        scratch_shapes=[*compute_scratch().values(), *reduce_scratch().values()],
        compiler_params=pltpu.CompilerParams(
            collective_id=0, has_side_effects=True, vmem_limit_bytes=60 * 1024 * 1024
        ),
        name="layer_back",
    )(*operands)


def store(*values):
    count = len(values)

    def kernel(*refs):
        sems = refs[2 * count]
        copies = [pltpu.make_async_copy(refs[i], refs[count + i], sems.at[i]) for i in range(count)]
        for copy in copies:
            copy.start()
        for copy in copies:
            copy.wait()

    return pl.pallas_call(
        kernel,
        out_shape=tuple(jax.ShapeDtypeStruct(value.shape, value.dtype) for value in values),
        in_specs=[pl.BlockSpec(memory_space=pltpu.VMEM)] * count,
        out_specs=(pl.BlockSpec(memory_space=pltpu.HBM),) * count,
        scratch_shapes=[pltpu.SemaphoreType.DMA((count,))],
        name="store",
    )(*values)


def per_device(
    nodes,
    edges,
    node_cotan,
    edge_cotan,
    edge_inner,
    edge_outer,
    node_inner,
    node_outer,
    edge_shift,
    edge_offset,
    edge_gain,
    node_shift,
    node_offset,
    node_gain,
    send_rows,
    senders,
    receivers,
):
    devices_all = lax.axis_size("region") * lax.axis_size("patch")
    edge_norm = 1.0 / math.sqrt(EDGES * devices_all)
    node_norm = 1.0 / math.sqrt(NODES * devices_all)
    vectors = (edge_shift, edge_offset, edge_gain, node_shift, node_offset, node_gain)
    grad_nodes, grad_edges, weights, vector_sums = layer(
        edge_norm,
        node_norm,
        nodes,
        edges,
        node_cotan,
        edge_cotan,
        edge_inner,
        edge_outer,
        node_inner,
        node_outer,
        *(vector.reshape(1, WIDTH) for vector in vectors),
        send_rows.reshape(2, SLOTS),
        senders.reshape(EDGES // 128, 128),
        receivers.reshape(EDGES // 128, 128),
    )
    grad_nodes, grad_edges, weights, vector_sums = store(grad_nodes, grad_edges, weights, vector_sums)
    return (grad_nodes, grad_edges, weights.reshape(-1), vector_sums.reshape(-1))


def solution(mesh):
    in_specs = (
        P(("region", "patch"), None),
        P(("region", "patch"), None),
        P(("region", "patch"), None),
        P(("region", "patch"), None),
        P(),
        P(),
        P(),
        P(),
        P(),
        P(),
        P(),
        P(),
        P(),
        P(),
        P("region", "patch", None, None),
        P(("region", "patch")),
        P(("region", "patch")),
    )
    out_specs = (
        P(("region", "patch"), None),
        P(("region", "patch"), None),
        P(("region", "patch")),
        P(),
    )
    return jax.shard_map(
        per_device, mesh=mesh, in_specs=in_specs, out_specs=out_specs, check_vma=False
    )
```
